512 devices in a mesh: px: 32 (over y, x), py: 16 (over z, core).
Axes of the slice: x: 4, y: 8, z: 8, core: 2. Of those that a mesh axis runs over, the one named last changes fastest.
Arguments:
- node_features: bfloat16 [262144, 192], P(('px', 'py')), may hold values from -6 to 6
- edge_source: int32 [512, 3072], P(('px', 'py')), may hold values from 0 to 767
- edge_target: int32 [512, 3072], P(('px', 'py')), may hold values from 0 to 512, as said below
- halo_send: int32 [512, 64], P(('px', 'py')), may hold values from 0 to 511
- edge_weight_in: bfloat16 [384, 192], replicated, may hold values from -0.3125 to 0.3125
- edge_bias: float32 [192], replicated, may hold values from -4 to 4
- edge_weight_out: bfloat16 [192, 192], replicated, may hold values from -0.4375 to 0.4375
- node_weight_in: bfloat16 [384, 192], replicated, may hold values from -0.3125 to 0.3125
- node_bias: float32 [192], replicated, may hold values from -4 to 4
- node_weight_out: bfloat16 [192, 192], replicated, may hold values from -0.4375 to 0.4375
- cluster_owner: int32 [262144, 1], P(('px', 'py')), may hold values from 0 to 15; in each aligned block of 512 rows (0 to 511, 512 to 1023, ...) at most 64 rows name the same one
- cluster_member: int32 [262144], P(('px', 'py')), may hold values from 0 to 63
- coarse_send: int32 [512, 16], P(('px', 'py')), may hold values from 0 to 63
- coarse_source: int32 [512, 384], P(('px', 'py')), may hold values from 0 to 127
- coarse_target: int32 [512, 384], P(('px', 'py')), may hold values from 0 to 64, as said below
- coarse_edge_in: bfloat16 [384, 192], replicated, may hold values from -0.3125 to 0.3125
- coarse_edge_bias: float32 [192], replicated, may hold values from -4 to 4
- coarse_edge_out: bfloat16 [192, 192], replicated, may hold values from -0.4375 to 0.4375
- coarse_node_in: bfloat16 [384, 192], replicated, may hold values from -0.3125 to 0.3125
- coarse_node_bias: float32 [192], replicated, may hold values from -4 to 4
- coarse_node_out: bfloat16 [192, 192], replicated, may hold values from -0.4375 to 0.4375
Outputs:
- node_updated: bfloat16 [262144, 192], P(('px', 'py'))
- cluster_updated: bfloat16 [32768, 192], P(('px', 'py'))
The draws below stay inside these ranges and needn't reach their ends.
Inputs may be any that keep to these rules, and one draw needn't show every extreme that they name: `edge_target`: each device's slots hold a target node of that device; padding slots hold 512 and stand only at the end of a device's list; at least three quarters of each device's slots are live and some device has no padding. `coarse_target`: each device's slots hold a target cluster of that device; padding slots hold 64 and stand only at the end of a device's list; at least three quarters of each device's slots are live and some device has no padding. `cluster_owner`: at most 64 nodes of one device have the same owner, and in every draw some device has exactly 64 nodes with one owner.
All inputs are finite; a program needn't handle non-finite values.
Results may differ from the reference program's by a relative error of at most 0.014.
Values may be sent and summed in bfloat16 or wider, within the bound.
No kernel may reach another device: no remote copies, remote signals or barrier semaphores. Data moves between devices by JAX's collectives and lax.ppermute only.
A program may use at most 64 MiB of HBM per device.

```python
import math
import jax
import jax.numpy as jnp
import numpy as np
from jax import lax

H = 192
NODE_DEV = 512
NBLOCK = 512
NODES = 262144
CLUST_DEV = 64
CLUSTERS = 32768
EDGE_DEV = 3072
E3_DEV = 384
HALO = 64
HALO3 = 16
OWNERS = 16
CAP = 64
N_PX = 32
N_PY = 16


def padded_targets(key, lists, top_index, length):
    first_key, second_key, third_key = jax.random.split(key, 3)
    targets = jax.random.randint(first_key, (lists, length), 0, top_index, dtype=jnp.int32)
    live_count = jax.random.randint(second_key, (lists, 1), length - length // 4, length + 1, dtype=jnp.int32)
    chosen = jax.random.randint(third_key, (), 0, lists, dtype=jnp.int32)
    row_index = lax.broadcasted_iota(jnp.int32, (lists, 1), 0)
    live_count = jnp.where(row_index == chosen, length, live_count)
    position = lax.broadcasted_iota(jnp.int32, (lists, length), 1)
    return jnp.where(position < live_count, targets, top_index).astype(jnp.int32)


def draw_edge_target(key, part):
    return padded_targets(jax.random.fold_in(key, 11), NBLOCK, NODE_DEV, EDGE_DEV)


def draw_coarse_target(key, part):
    return padded_targets(jax.random.fold_in(key, 23), NBLOCK, CLUST_DEV, E3_DEV)


def with_ends(values, stream_key, least, largest):
    shape = values.shape
    place = [jax.random.randint(jax.random.fold_in(stream_key, axis), (), 0, shape[axis]) for axis in range(len(shape))]
    values = values.at[tuple(place)].set(least)
    longest = shape.index(max(shape))
    place[longest] = (place[longest] + 1) % shape[longest]
    return values.at[tuple(place)].set(largest)


def block_scale(rng, shape, cuts, smallest, high):
    factor_of = 1.0
    for dim, blocks in cuts:
        heights = jax.random.uniform(jax.random.fold_in(jax.random.fold_in(rng, 6), dim), (blocks,), jnp.float32, smallest / len(cuts), high / len(cuts))
        factor_of = factor_of * jnp.repeat(jnp.exp(heights), shape[dim] // blocks).reshape((-1,) + (1,) * (len(shape) - 1 - dim))
    return factor_of


def rank_bounds(number_of, skew):
    weights = [(1 << 20) // math.isqrt(grade ** skew) + 1 for grade in range(1, number_of + 1)]
    scale = 1 + sum(weights) // (1 << 30)
    return np.cumsum(np.array([max(1, weight // scale) for weight in weights]))


def skewed_ids(rng, dims, number_of, lean):
    grid = rank_bounds(number_of, lean)
    lot = jax.random.randint(jax.random.fold_in(rng, 1), dims, 0, int(grid[number_of - 1]))
    rank = jnp.searchsorted(jnp.asarray(grid, jnp.int32), lot, side="right")
    return jax.random.permutation(jax.random.fold_in(rng, 2), number_of)[rank].astype(jnp.int32)


def deal_out(rng, own, number, rows, amount, top, limit, skew):
    order = jax.random.permutation(rng, amount)
    packed, ordinary = shares(amount, rows * top, limit, skew, True), shares(amount, rows * top, limit, skew, False)
    places = jnp.arange(amount)

    def named(sizes, rotation):
        used = int((sizes > 0).sum())
        fixed = max(1, used // 4)
        passed = fixed + (places - fixed + rotation * (used - fixed)) % max(1, amount - fixed)
        return jnp.zeros((amount,), jnp.int32).at[order[jnp.where(places < fixed, places, passed)]].set(jnp.asarray(sizes, jnp.int32))

    sizes = jnp.where(number % 4 == 0, named(packed, number // 4), named(ordinary, number - number // 4 - 1))
    mixed = jax.random.permutation(jax.random.fold_in(own, 3), amount)
    giver, sink = mixed[0:amount // 2 * 2:2], mixed[1:amount // 2 * 2:2]
    margin = jnp.minimum(sizes[giver] - 1, limit - sizes[sink]) // 2
    margin = jnp.where((giver == order[0]) | (sink == order[0]) | (sizes[sink] == 0), 0, jnp.maximum(margin, 0))
    passed = jax.random.randint(jax.random.fold_in(own, 4), (amount // 2,), 0, 1 << 20) % (margin + 1)
    sizes = sizes.at[giver].add(-passed).at[sink].add(passed)
    members = jnp.searchsorted(jnp.cumsum(sizes), jnp.arange(rows * top), side="right").astype(jnp.int32)
    listing = members.reshape(top, rows).T
    listing = listing[jax.random.permutation(jax.random.fold_in(own, 1), rows)]
    rotation = jax.random.randint(jax.random.fold_in(own, 2), (rows, 1), 0, top)
    return jnp.take_along_axis(listing, (jnp.arange(top)[None, :] + rotation) % top, axis=1)


def shares(number_of, total, reach, skew, full):
    loads = [(1 << 20) // math.isqrt(rank ** skew) + 1 for rank in range(1, number_of + 1)]
    largest = reach if full else min(reach, max(-(-total // number_of), total * loads[0] // sum(loads)))
    least = 1 if total - largest >= number_of - 1 else 0
    given, surplus = [largest] + [least] * (number_of - 1), total - largest - least * (number_of - 1)
    while surplus > 0:
        candidates = [i for i in range(1, number_of) if given[i] < largest] or [i for i in range(1, number_of) if given[i] < reach]
        pool, remaining = sum([loads[i] for i in candidates]), surplus
        for i in candidates:
            more = min(reach - given[i], max(1, remaining * loads[i] // pool), surplus)
            given[i] = given[i] + more
            surplus = surplus - more
    return np.array(given)


def normal_values(own_key, dims, deviation, bound, shards=(), kind=jnp.bfloat16):
    values = deviation * jax.random.normal(own_key, dims, jnp.float32)
    if shards:
        values = values * block_scale(own_key, dims, shards, -0.22, 0.18)
    return jnp.clip(values, -bound, bound).astype(kind)


def setup_inputs(seed: int = 0) -> dict:
    streams_of = jax.random.split(jax.random.key(seed), 22)
    node_features = normal_values(streams_of[0], (NODES, H), 1.0, 6.0, ((0, 512),))
    edge_source = with_ends(jax.random.randint(streams_of[1], (NBLOCK, EDGE_DEV), 0, NODE_DEV + 4 * HALO), jax.random.fold_in(streams_of[1], 1), 0, (NODE_DEV + 4 * HALO) - 1).astype(jnp.int32)
    edge_target = draw_edge_target(jax.random.fold_in(streams_of[21], 71), 0)
    halo_send = with_ends(jax.random.randint(streams_of[3], (NBLOCK, HALO), 0, NODE_DEV), jax.random.fold_in(streams_of[3], 1), 0, NODE_DEV - 1).astype(jnp.int32)
    edge_weight_in = normal_values(streams_of[4], (2 * H, H), (2 * H) ** -0.5, 0.3125)
    edge_bias = normal_values(streams_of[5], (H,), 1.0, 4.0, (), jnp.float32)
    edge_weight_out = normal_values(streams_of[6], (H, H), H ** -0.5, 0.4375)
    node_weight_in = normal_values(streams_of[7], (2 * H, H), (2 * H) ** -0.5, 0.3125)
    node_bias = normal_values(streams_of[8], (H,), 1.0, 4.0, (), jnp.float32)
    node_weight_out = normal_values(streams_of[9], (H, H), H ** -0.5, 0.4375)
    cluster_owner_keys = jax.random.split(jax.random.fold_in(streams_of[10], 1), NODES // NODE_DEV)
    cluster_owner_turns = jax.random.permutation(jax.random.fold_in(streams_of[10], 3), NODES // NODE_DEV)
    cluster_owner = jax.vmap(lambda own, number: deal_out(jax.random.fold_in(streams_of[10], 2), own, number, NODE_DEV, OWNERS, 1, CAP, 1))(cluster_owner_keys, cluster_owner_turns).reshape((NODES, 1))
    cluster_member = with_ends(skewed_ids(streams_of[11], (NODES,), CLUST_DEV, 2), jax.random.fold_in(streams_of[11], 3), 0, CLUST_DEV - 1).astype(jnp.int32)
    coarse_send = with_ends(jax.random.randint(streams_of[12], (NBLOCK, HALO3), 0, CLUST_DEV), jax.random.fold_in(streams_of[12], 1), 0, CLUST_DEV - 1).astype(jnp.int32)
    coarse_source = with_ends(jax.random.randint(streams_of[13], (NBLOCK, E3_DEV), 0, CLUST_DEV + 4 * HALO3), jax.random.fold_in(streams_of[13], 1), 0, (CLUST_DEV + 4 * HALO3) - 1).astype(jnp.int32)
    coarse_target = draw_coarse_target(jax.random.fold_in(streams_of[21], 71), 0)
    coarse_edge_in = normal_values(streams_of[15], (2 * H, H), (2 * H) ** -0.5, 0.3125)
    coarse_edge_bias = normal_values(streams_of[16], (H,), 1.0, 4.0, (), jnp.float32)
    coarse_edge_out = normal_values(streams_of[17], (H, H), H ** -0.5, 0.4375)
    coarse_node_in = normal_values(streams_of[18], (2 * H, H), (2 * H) ** -0.5, 0.3125)
    coarse_node_bias = normal_values(streams_of[19], (H,), 1.0, 4.0, (), jnp.float32)
    coarse_node_out = normal_values(streams_of[20], (H, H), H ** -0.5, 0.4375)
    return dict(node_features=node_features, edge_source=edge_source, edge_target=edge_target, halo_send=halo_send, edge_weight_in=edge_weight_in, edge_bias=edge_bias, edge_weight_out=edge_weight_out, node_weight_in=node_weight_in, node_bias=node_bias, node_weight_out=node_weight_out, cluster_owner=cluster_owner, cluster_member=cluster_member, coarse_send=coarse_send, coarse_source=coarse_source, coarse_target=coarse_target, coarse_edge_in=coarse_edge_in, coarse_edge_bias=coarse_edge_bias, coarse_edge_out=coarse_edge_out, coarse_node_in=coarse_node_in, coarse_node_bias=coarse_node_bias, coarse_node_out=coarse_node_out)


def normed(values):
    center = values - lax.optimization_barrier(jnp.mean(values, axis=-1, keepdims=True))
    return center * lax.rsqrt(lax.optimization_barrier(jnp.mean(center * center, axis=-1, keepdims=True)) + 1e-05)

def neighbour_table(send, per_device, blocks):
    device = jnp.arange(blocks).astype(jnp.int32)
    first_pos = device // N_PY
    second_pos = device % N_PY
    own_ids = (device[:, None] * per_device + jnp.arange(per_device).astype(jnp.int32)[None, :]).astype(jnp.int32)
    columns_list = [own_ids]
    for offset_first, offset_second in ((-1, 0), (1, 0), (0, -1), (0, 1)):
        near_first = first_pos + offset_first
        near_second = second_pos + offset_second
        inside = (near_first >= 0) & (near_first < N_PX) & (near_second >= 0) & (near_second < N_PY)
        near_device = (jnp.clip(near_first, 0, N_PX - 1) * N_PY + jnp.clip(near_second, 0, N_PY - 1)).astype(jnp.int32)
        global_ids = (near_device[:, None] * per_device + send[near_device]).astype(jnp.int32)
        columns_list.append(jnp.where(inside[:, None], global_ids, blocks * per_device).astype(jnp.int32))
    return jnp.concatenate(columns_list, axis=1).astype(jnp.int32)

def level_round(features, sources, targets, send, per_device, weights):
    weight_in, bias, weight_out, node_in, node_bias, node_out = weights
    blocks = sources.shape[0]
    width = features.shape[1]
    lookup = neighbour_table(send, per_device, blocks)
    global_sources = jnp.take_along_axis(lookup, sources, axis=1).astype(jnp.int32)
    padded = jnp.concatenate([features, jnp.zeros((1, width), jnp.bfloat16)], axis=0)

    def one_device(pieces):
        local_rows, source_ids, target_ids = pieces
        paired = jnp.concatenate([jnp.take(padded, source_ids, axis=0), jnp.take(local_rows, jnp.minimum(target_ids, per_device - 1), axis=0)], axis=1)
        hidden = jax.nn.silu(jnp.dot(paired, weight_in, preferred_element_type=jnp.float32) + bias).astype(jnp.bfloat16)
        message = normed(jnp.dot(hidden, weight_out, preferred_element_type=jnp.float32))
        totals = jnp.zeros((per_device, width), jnp.float32).at[target_ids].add(message, mode='drop')
        joined = jnp.concatenate([local_rows, totals.astype(jnp.bfloat16)], axis=1)
        node_hidden = jax.nn.silu(jnp.dot(joined, node_in, preferred_element_type=jnp.float32) + node_bias).astype(jnp.bfloat16)
        return (local_rows.astype(jnp.float32) + normed(jnp.dot(node_hidden, node_out, preferred_element_type=jnp.float32))).astype(jnp.bfloat16)
    result = lax.map(one_device, (features.reshape(blocks, per_device, width), global_sources, targets))
    return result.reshape(features.shape)

def reference(node_features, edge_source, edge_target, halo_send, edge_weight_in, edge_bias, edge_weight_out, node_weight_in, node_bias, node_weight_out, cluster_owner, cluster_member, coarse_send, coarse_source, coarse_target, coarse_edge_in, coarse_edge_bias, coarse_edge_out, coarse_node_in, coarse_node_bias, coarse_node_out):
    node_updated = level_round(node_features, edge_source, edge_target, halo_send, NODE_DEV, (edge_weight_in, edge_bias, edge_weight_out, node_weight_in, node_bias, node_weight_out))
    device = (jnp.arange(NODES) // NODE_DEV).astype(jnp.int32)
    position = ((device // N_PY * N_PY + cluster_owner[:, 0]) * CLUST_DEV + cluster_member).astype(jnp.int32)
    pooled = jax.ops.segment_sum(node_updated.astype(jnp.float32), position, num_segments=CLUSTERS)
    counts = jax.ops.segment_sum(jnp.ones((NODES,), jnp.float32), position, num_segments=CLUSTERS)
    coarse = (pooled / jnp.maximum(counts, 1.0)[:, None]).astype(jnp.bfloat16)
    cluster_updated = level_round(coarse, coarse_source, coarse_target, coarse_send, CLUST_DEV, (coarse_edge_in, coarse_edge_bias, coarse_edge_out, coarse_node_in, coarse_node_bias, coarse_node_out))
    return (node_updated, cluster_updated)
```

```python
import jax
import jax.numpy as jnp
from jax import lax
from jax.experimental import pallas as pl
from jax.experimental.pallas import tpu as pltpu
from jax.sharding import PartitionSpec as P

WIDTH = 192
CLUST_DEV = 64
OWNERS = 16
BLOCK = 512
F32, BF16, I32 = jnp.float32, jnp.bfloat16, jnp.int32


def nn(a, b):
    return jnp.dot(a, b, preferred_element_type=F32)


def nt(a, b):
    return lax.dot_general(a, b, (((1,), (1,)), ((), ())), preferred_element_type=F32)


def one_hot(ids, count):
    n = ids.shape[1]
    pieces = []
    for start in range(0, count, 256):
        rows = min(256, count - start)
        row = lax.broadcasted_iota(I32, (rows, n), 0).astype(F32).astype(BF16)
        here = (ids - start).astype(F32).astype(BF16)
        pieces.append(jnp.where(row == here, 1.0, 0.0).astype(BF16))
    return pieces[0] if len(pieces) == 1 else jnp.concatenate(pieces, axis=0)


def half_silu(half):
    return half * jnp.tanh(half) + half


def normed(values):
    center = values - jnp.mean(values, axis=0, keepdims=True)
    return center * lax.rsqrt(jnp.mean(center * center, axis=0, keepdims=True) + 1e-05)


def column(row, count):
    at = lax.broadcasted_iota(I32, (count, count), 0) == lax.broadcasted_iota(
        I32, (count, count), 1
    )
    return jnp.sum(jnp.where(at, row.astype(F32), 0.0), axis=1, keepdims=True).astype(I32)


def pick(send, table):
    count, total = send.shape[1], table.shape[1]
    ids = column(send, count)
    chosen = jnp.where(
        lax.broadcasted_iota(I32, (count, total), 1) == ids, 1.0, 0.0
    ).astype(BF16)
    return nt(chosen, table).astype(BF16)


def inside_flags():
    i, j = lax.axis_index("px"), lax.axis_index("py")
    return (i > 0, i < lax.axis_size("px") - 1, j > 0, j < lax.axis_size("py") - 1)


def halo_rows(refs):
    rows = []
    for ref, inside in zip(refs, inside_flags()):
        rows.append(jnp.where(inside, ref[...].astype(F32), 0.0).astype(BF16))
    return jnp.concatenate(rows, axis=0)


def pick_kernel(send_ref, table_ref, out_ref):
    out_ref[...] = pick(send_ref[...], table_ref[...])


def node_stage(features, incoming, node_in, node_bias, node_out):
    joined = jnp.concatenate([features, incoming.astype(BF16)], axis=0)
    hidden = half_silu(0.5 * (nn(node_in, joined) + node_bias)).astype(BF16)
    return features.astype(F32) + normed(nn(node_out, hidden))


def fine_kernel(
    feat_ref,
    h0,
    h1,
    h2,
    h3,
    src_ref,
    tgt_ref,
    win_ref,
    bias_ref,
    wout_ref,
    nin_ref,
    nbias_ref,
    nout_ref,
    owner_ref,
    member_ref,
    updated_ref,
    payload_ref,
    picks_ref,
    totals_ref,
):
    nodes = feat_ref.shape[1]
    features = feat_ref[...]
    w_top, w_bot = win_ref[:, :WIDTH], win_ref[:, WIDTH:]
    rim = halo_rows((h0, h1, h2, h3))
    lookups = nodes + rim.shape[0]
    picks_ref[:, :nodes] = (0.5 * nn(w_top, features)).astype(BF16)
    picks_ref[:, nodes:lookups] = (0.5 * nt(w_top, rim)).astype(BF16)
    picks_ref[:, lookups:] = (0.5 * nn(w_bot, features)).astype(BF16)
    bias = 0.5 * bias_ref[...]
    w_out = wout_ref[...].astype(F32).T.astype(BF16)
    totals_ref[...] = jnp.zeros_like(totals_ref)

    def block(step, carry):
        at = pl.ds(pl.multiple_of(step * BLOCK, BLOCK), BLOCK)
        from_source = one_hot(src_ref[:, at], lookups)
        to_target = one_hot(tgt_ref[:, at], nodes)
        half = nn(picks_ref[:, :lookups], from_source) + nn(picks_ref[:, lookups:], to_target)
        hidden = half_silu(half + bias).astype(BF16)
        message = normed(nn(w_out, hidden)).astype(BF16)
        totals_ref[...] += nt(message, to_target)
        return carry

    lax.fori_loop(0, src_ref.shape[1] // BLOCK, block, 0, unroll=True)

    n_out = nout_ref[...].astype(F32).T.astype(BF16)
    updated = node_stage(features, totals_ref[...], nin_ref[...], nbias_ref[...], n_out)
    updated = updated.astype(BF16)
    updated_ref[...] = updated

    position = owner_ref[...] * CLUST_DEV + member_ref[...]
    counted = jnp.concatenate([updated, jnp.ones((16, nodes), BF16)], axis=0)
    for pair in range(OWNERS // 2):
        member_of = jnp.where(
            lax.broadcasted_iota(I32, (2 * CLUST_DEV, nodes), 0) + pair * 2 * CLUST_DEV
            == position,
            1.0,
            0.0,
        ).astype(BF16)
        pooled = nt(counted, member_of)
        half = WIDTH // 2
        top, low, count = pooled[:half], pooled[half:WIDTH], pooled[WIDTH : WIDTH + 8]
        left = lax.broadcasted_iota(I32, (half, 2 * CLUST_DEV), 1) < CLUST_DEV
        payload_ref[2 * pair, :half, :] = jnp.where(
            left, top, pltpu.roll(low, CLUST_DEV, 1)
        ).astype(BF16)
        payload_ref[2 * pair, half:, :] = count.astype(BF16)
        payload_ref[2 * pair + 1, :half, :] = jnp.where(
            left, pltpu.roll(top, CLUST_DEV, 1), low
        ).astype(BF16)
        payload_ref[2 * pair + 1, half:, :] = pltpu.roll(count, CLUST_DEV, 1).astype(BF16)


def coarse_kernel(parts_ref, send_ref, coarse_ref, shared_ref):
    total = jnp.sum(parts_ref[...].astype(F32), axis=0)
    half = WIDTH // 2
    sums = jnp.concatenate([total[:half], pltpu.roll(total[:half], CLUST_DEV, 1)], axis=0)
    counts = total[half : half + 1]
    coarse = (sums / jnp.maximum(counts, 1.0)).astype(BF16)[:, :CLUST_DEV]
    coarse_ref[...] = coarse
    shared_ref[...] = pick(send_ref[...], coarse)


def level3_kernel(
    feat_ref,
    h0,
    h1,
    h2,
    h3,
    src_ref,
    tgt_ref,
    win_ref,
    bias_ref,
    wout_ref,
    nin_ref,
    nbias_ref,
    nout_ref,
    updated_ref,
):
    nodes = feat_ref.shape[1]
    features = feat_ref[...]
    w_top, w_bot = win_ref[:, :WIDTH], win_ref[:, WIDTH:]
    rim = halo_rows((h0, h1, h2, h3))
    lookups = nodes + rim.shape[0]
    from_source = one_hot(src_ref[...], lookups)
    to_target = one_hot(tgt_ref[...], nodes)
    half = (
        nn((0.5 * nn(w_top, features)).astype(BF16), from_source[:nodes])
        + nn((0.5 * nt(w_top, rim)).astype(BF16), from_source[nodes:])
        + nn((0.5 * nn(w_bot, features)).astype(BF16), to_target)
    )
    hidden = half_silu(half + 0.5 * bias_ref[...]).astype(BF16)
    w_out = wout_ref[...].astype(F32).T.astype(BF16)
    message = normed(nn(w_out, hidden)).astype(BF16)
    totals = nt(message, to_target)
    n_out = nout_ref[...].astype(F32).T.astype(BF16)
    updated = node_stage(features, totals, nin_ref[...], nbias_ref[...], n_out)
    wide = jnp.concatenate([updated, jnp.zeros_like(updated)], axis=1)
    updated_ref[...] = wide.T[:nodes].astype(BF16)


def exchange(shared):
    found = []
    for axis in ("px", "py"):
        count = lax.axis_size(axis)
        ahead = [(k, (k + 1) % count) for k in range(count)]
        found.append(lax.ppermute(shared, axis, ahead))
        found.append(lax.ppermute(shared, axis, [(b, a) for a, b in ahead]))
    return found


def call(kernel, outs, scratch, *args):
    return pl.pallas_call(
        kernel,
        out_shape=[jax.ShapeDtypeStruct(shape, BF16) for shape in outs],
        scratch_shapes=scratch,
        name=kernel.__name__,
    )(*args)


def body(
    node_features,
    edge_source,
    edge_target,
    halo_send,
    edge_weight_in,
    edge_bias,
    edge_weight_out,
    node_weight_in,
    node_bias,
    node_weight_out,
    cluster_owner,
    cluster_member,
    coarse_send,
    coarse_source,
    coarse_target,
    coarse_edge_in,
    coarse_edge_bias,
    coarse_edge_out,
    coarse_node_in,
    coarse_node_bias,
    coarse_node_out,
):
    nodes = node_features.shape[0]
    features = node_features.T
    (shared,) = call(pick_kernel, [(halo_send.shape[1], WIDTH)], [], halo_send, features)
    rims = exchange(shared)
    updated, payload = call(
        fine_kernel,
        [(WIDTH, nodes), (OWNERS, WIDTH // 2 + 8, 2 * CLUST_DEV)],
        [pltpu.VMEM((WIDTH, 1280), BF16), pltpu.VMEM((WIDTH, nodes), F32)],
        features,
        *rims,
        edge_source,
        edge_target,
        edge_weight_in.T,
        edge_bias[:, None],
        edge_weight_out,
        node_weight_in.T,
        node_bias[:, None],
        node_weight_out,
        cluster_owner.reshape(1, nodes),
        cluster_member.reshape(1, nodes),
    )
    parts = lax.all_to_all(payload, "py", 0, 0, tiled=True)
    coarse, coarse_shared = call(
        coarse_kernel,
        [(WIDTH, CLUST_DEV), (coarse_send.shape[1], WIDTH)],
        [],
        parts,
        coarse_send,
    )
    coarse_rims = exchange(coarse_shared)
    (cluster_updated,) = call(
        level3_kernel,
        [(CLUST_DEV, WIDTH)],
        [],
        coarse,
        *coarse_rims,
        coarse_source,
        coarse_target,
        coarse_edge_in.T,
        coarse_edge_bias[:, None],
        coarse_edge_out,
        coarse_node_in.T,
        coarse_node_bias[:, None],
        coarse_node_out,
    )
    return updated.T, cluster_updated


def solution(mesh):
    split, whole = P(("px", "py"), None), P()
    return jax.shard_map(
        body,
        mesh=mesh,
        in_specs=(split,) * 4
        + (whole,) * 6
        + (split, P(("px", "py")))
        + (split,) * 3
        + (whole,) * 6,
        out_specs=(split, split),
        check_vma=False,
    )
```

```python
import jax
import jax.numpy as jnp
from jax import lax
from jax.experimental import pallas as pl
from jax.experimental.pallas import tpu as pltpu
from jax.sharding import PartitionSpec as P

WIDTH = 192
CLUST_DEV = 64
OWNERS = 16
BLOCK = 1024
F32, BF16, I32, I16 = jnp.float32, jnp.bfloat16, jnp.int32, jnp.int16


def nn(a, b):
    return jnp.dot(a, b, preferred_element_type=F32)


def nt(a, b):
    return lax.dot_general(a, b, (((1,), (1,)), ((), ())), preferred_element_type=F32)


def one_hot_rows(ids, count):
    row = lax.broadcasted_iota(I32, (count, ids.shape[1]), 0).astype(I16)
    return jnp.where(row == ids.astype(I16), jnp.ones_like(row, BF16), jnp.zeros_like(row, BF16))


def one_hot_lanes(ids, count):
    shape = (ids.shape[0], count)
    lane = lax.broadcasted_iota(I32, shape, 1).astype(I16)
    wide = jnp.broadcast_to(ids, (ids.shape[0], 128)).astype(I16)
    found = lane == jnp.tile(wide, (1, count // 128))
    return jnp.where(found, jnp.ones_like(lane, BF16), jnp.zeros_like(lane, BF16))


def half_silu(half):
    return half * jnp.tanh(half) + half


def normed(values, axis):
    center = values - jnp.mean(values, axis=axis, keepdims=True)
    return center * lax.rsqrt(jnp.mean(center * center, axis=axis, keepdims=True) + 1e-05)


def column(row, count):
    shape = (count, count)
    at = lax.broadcasted_iota(I32, shape, 0) == lax.broadcasted_iota(I32, shape, 1)
    return jnp.sum(jnp.where(at, row, 0.0), axis=1, keepdims=True)


def chooser(send, total):
    count = send.shape[1]
    ids = column(send.astype(F32), count).astype(I32)
    lane = lax.broadcasted_iota(I32, (count, total), 1)
    return jnp.where(lane == ids, 1.0, 0.0).astype(BF16)


def inside_flags():
    i, j = lax.axis_index("px"), lax.axis_index("py")
    return (i > 0, i < lax.axis_size("px") - 1, j > 0, j < lax.axis_size("py") - 1)


def halo_rows(refs):
    rows = []
    for ref, inside in zip(refs, inside_flags()):
        rows.append(jnp.where(inside, ref[...].astype(F32), 0.0).astype(BF16))
    return jnp.concatenate(rows, axis=0)


def pick_kernel(send_ref, table_ref, out_ref):
    out_ref[...] = nt(chooser(send_ref[...], table_ref.shape[1]), table_ref[...]).astype(BF16)


def prepare_kernel(
    send3_ref,
    bias_ref,
    nbias_ref,
    wout_ref,
    nout_ref,
    feat_ref,
    win_ref,
    own_ref,
    into_ref,
    cols_ref,
    wide_ref,
    chosen_ref,
):
    chosen_ref[...] = chooser(send3_ref[...], CLUST_DEV)
    features = feat_ref[...]
    own_ref[...] = (0.5 * nn(win_ref[:, :WIDTH], features)).astype(BF16)
    into_ref[...] = (0.5 * nn(win_ref[:, WIDTH:], features)).astype(BF16)
    wide_ref[0] = wout_ref[...].astype(F32).T.astype(BF16)
    wide_ref[1] = nout_ref[...].astype(F32).T.astype(BF16)
    cols_ref[0] = jnp.broadcast_to(column(0.5 * bias_ref[...], WIDTH), (WIDTH, 128))
    cols_ref[1] = jnp.broadcast_to(column(0.5 * nbias_ref[...], WIDTH), (WIDTH, 128))


def fine_kernel(
    feat_ref,
    own_ref,
    into_ref,
    cols_ref,
    wide_ref,
    h0,
    h1,
    h2,
    h3,
    src_ref,
    tgt_ref,
    win_ref,
    nin_ref,
    owner_ref,
    member_ref,
    updated_ref,
    payload_ref,
    picks_ref,
    totals_ref,
):
    nodes = feat_ref.shape[1]
    rim = halo_rows((h0, h1, h2, h3))
    lookups = nodes + rim.shape[0]
    picks_ref[:, :nodes] = own_ref[...]
    picks_ref[:, nodes:lookups] = (0.5 * nt(win_ref[:, :WIDTH], rim)).astype(BF16)
    picks_ref[:, lookups:] = into_ref[...]
    for step in range(src_ref.shape[1] // BLOCK):
        at = pl.ds(step * BLOCK, BLOCK)
        from_source = one_hot_rows(src_ref[:, at], lookups)
        to_target = one_hot_rows(tgt_ref[:, at], nodes)
        half = nn(picks_ref[...], jnp.concatenate([from_source, to_target], axis=0))
        hidden = half_silu(half + jnp.tile(cols_ref[0], (1, BLOCK // 128))).astype(BF16)
        message = normed(nn(wide_ref[0], hidden), 0).astype(BF16)
        added = nt(message, to_target)
        if step == 0:
            totals_ref[...] = added
        else:
            totals_ref[...] += added

    features = feat_ref[...]
    joined = jnp.concatenate([features, totals_ref[...].astype(BF16)], axis=0)
    half = 0.5 * nn(nin_ref[...], joined) + jnp.tile(cols_ref[1], (1, nodes // 128))
    updated = features.astype(F32) + normed(nn(wide_ref[1], half_silu(half).astype(BF16)), 0)
    updated = updated.astype(BF16)
    updated_ref[...] = updated

    position = owner_ref[...] * CLUST_DEV + member_ref[...]
    counted = jnp.concatenate([updated, jnp.ones((16, nodes), BF16)], axis=0)
    member_of = one_hot_rows(position, OWNERS * CLUST_DEV)
    pooled = nt(counted, member_of)
    for pair in range(OWNERS // 2):
        part = pooled[:, pair * 2 * CLUST_DEV : (pair + 1) * 2 * CLUST_DEV]
        half = WIDTH // 2
        top, low, count = part[:half], part[half:WIDTH], part[WIDTH : WIDTH + 8]
        left = lax.broadcasted_iota(I32, (half, 2 * CLUST_DEV), 1) < CLUST_DEV
        payload_ref[2 * pair, :half, :] = jnp.where(
            left, top, pltpu.roll(low, CLUST_DEV, 1)
        ).astype(BF16)
        payload_ref[2 * pair, half:, :] = count.astype(BF16)
        payload_ref[2 * pair + 1, :half, :] = jnp.where(
            left, pltpu.roll(top, CLUST_DEV, 1), low
        ).astype(BF16)
        payload_ref[2 * pair + 1, half:, :] = pltpu.roll(count, CLUST_DEV, 1).astype(BF16)


def coarse_kernel(parts_ref, chosen_ref, coarse_ref, shared_ref):
    total = jnp.sum(parts_ref[...].astype(F32), axis=0)
    half = WIDTH // 2
    sums = jnp.concatenate([total[:half], pltpu.roll(total[:half], CLUST_DEV, 1)], axis=0)
    counts = total[half : half + 1]
    coarse = (sums / jnp.maximum(counts, 1.0)).astype(BF16)[:, :CLUST_DEV]
    coarse_ref[...] = coarse
    shared_ref[...] = nt(chosen_ref[...], coarse).astype(BF16)


def prepare3_kernel(
    src_ref,
    tgt_ref,
    bias_ref,
    nbias_ref,
    wout_ref,
    nout_ref,
    feat_ref,
    win_ref,
    half_ref,
    around_ref,
    target_ref,
    cols_ref,
    wide_ref,
):
    features = feat_ref[...]
    nodes = features.shape[1]
    own = (0.5 * nn(win_ref[:, :WIDTH], features)).astype(BF16)
    into = (0.5 * nn(win_ref[:, WIDTH:], features)).astype(BF16)
    from_own = one_hot_rows(src_ref[...], nodes)
    to_target = one_hot_rows(tgt_ref[...], nodes)
    target_ref[...] = to_target
    around_ref[...] = one_hot_rows(src_ref[...] - nodes, around_ref.shape[0])
    half_ref[...] = nn(own, from_own) + nn(into, to_target) + column(0.5 * bias_ref[...], WIDTH)
    wide_ref[0] = wout_ref[...].astype(F32).T.astype(BF16)
    wide_ref[1] = nout_ref[...].astype(F32).T.astype(BF16)
    cols_ref[...] = jnp.broadcast_to(column(0.5 * nbias_ref[...], WIDTH), (WIDTH, nodes))


def level3_kernel(
    feat_ref,
    half_ref,
    around_ref,
    target_ref,
    cols_ref,
    wide_ref,
    h0,
    h1,
    h2,
    h3,
    win_ref,
    nin_ref,
    updated_ref,
):
    features = feat_ref[...]
    nodes = features.shape[1]
    rim = halo_rows((h0, h1, h2, h3))
    near = (0.5 * nt(win_ref[:, :WIDTH], rim)).astype(BF16)
    hidden = half_silu(half_ref[...] + nn(near, around_ref[...])).astype(BF16)
    message = normed(nn(wide_ref[0], hidden), 0).astype(BF16)
    totals = nt(message, target_ref[...])
    joined = jnp.concatenate([features, totals.astype(BF16)], axis=0)
    hidden = half_silu(0.5 * nn(nin_ref[...], joined) + cols_ref[...]).astype(BF16)
    updated = features.astype(F32) + normed(nn(wide_ref[1], hidden), 0)
    wide = jnp.concatenate([updated, jnp.zeros_like(updated)], axis=1)
    updated_ref[...] = wide.T[:nodes].astype(BF16)


def exchange(shared):
    found = []
    for axis in ("px", "py"):
        count = lax.axis_size(axis)
        ahead = [(k, (k + 1) % count) for k in range(count)]
        found.append(lax.ppermute(shared, axis, ahead))
        found.append(lax.ppermute(shared, axis, [(b, a) for a, b in ahead]))
    return found


def call(kernel, outs, scratch, *args, loose=()):
    held = pl.BlockSpec(memory_space=pltpu.VMEM)
    return pl.pallas_call(
        kernel,
        out_shape=[space(shape, kind) for space, shape, kind in outs],
        in_specs=[held] * (len(loose) + len(args)),
        out_specs=[held] * len(outs),
        scratch_shapes=scratch,
        name=kernel.__name__,
    )(*loose, *[pltpu.with_memory_space_constraint(arg, pltpu.VMEM) for arg in args])


def body(
    node_features,
    edge_source,
    edge_target,
    halo_send,
    edge_weight_in,
    edge_bias,
    edge_weight_out,
    node_weight_in,
    node_bias,
    node_weight_out,
    cluster_owner,
    cluster_member,
    coarse_send,
    coarse_source,
    coarse_target,
    coarse_edge_in,
    coarse_edge_bias,
    coarse_edge_out,
    coarse_node_in,
    coarse_node_bias,
    coarse_node_out,
):
    nodes = node_features.shape[0]
    features = node_features.T
    (shared,) = call(
        pick_kernel,
        [(pltpu.VMEM, (halo_send.shape[1], WIDTH), BF16)],
        [],
        loose=(halo_send, features),
    )
    rims = exchange(shared)
    own, into, cols, wide, chosen = call(
        prepare_kernel,
        [(pltpu.VMEM, (WIDTH, nodes), BF16)] * 2
        + [
            (pltpu.VMEM, (2, WIDTH, 128), F32),
            (pltpu.VMEM, (2, WIDTH, WIDTH), BF16),
            (pltpu.VMEM, (coarse_send.shape[1], CLUST_DEV), BF16),
        ],
        [],
        features,
        edge_weight_in.T,
        loose=(coarse_send, edge_bias[None], node_bias[None], edge_weight_out, node_weight_out),
    )
    updated, payload = call(
        fine_kernel,
        [
            (jax.ShapeDtypeStruct, (WIDTH, nodes), BF16),
            (pltpu.VMEM, (OWNERS, WIDTH // 2 + 8, 2 * CLUST_DEV), BF16),
        ],
        [pltpu.VMEM((WIDTH, 1280), BF16), pltpu.VMEM((WIDTH, nodes), F32)],
        features,
        own,
        into,
        cols,
        wide,
        *rims,
        edge_source,
        edge_target,
        edge_weight_in.T,
        node_weight_in.T,
        cluster_owner.reshape(1, nodes),
        cluster_member.reshape(1, nodes),
    )
    parts = lax.all_to_all(payload, "py", 0, 0, tiled=True)
    coarse, coarse_shared = call(
        coarse_kernel,
        [
            (pltpu.VMEM, (WIDTH, CLUST_DEV), BF16),
            (pltpu.VMEM, (coarse_send.shape[1], WIDTH), BF16),
        ],
        [],
        parts,
        chosen,
    )
    coarse_rims = exchange(coarse_shared)
    links = coarse_source.shape[1]
    prepared = call(
        prepare3_kernel,
        [
            (pltpu.VMEM, (WIDTH, links), F32),
            (pltpu.VMEM, (4 * coarse_send.shape[1], links), BF16),
            (pltpu.VMEM, (CLUST_DEV, links), BF16),
            (pltpu.VMEM, (WIDTH, CLUST_DEV), F32),
            (pltpu.VMEM, (2, WIDTH, WIDTH), BF16),
        ],
        [],
        coarse,
        coarse_edge_in.T,
        loose=(
            coarse_source,
            coarse_target,
            coarse_edge_bias[None],
            coarse_node_bias[None],
            coarse_edge_out,
            coarse_node_out,
        ),
    )
    (cluster_updated,) = call(
        level3_kernel,
        [(jax.ShapeDtypeStruct, (CLUST_DEV, WIDTH), BF16)],
        [],
        coarse,
        *prepared,
        *coarse_rims,
        coarse_edge_in.T,
        coarse_node_in.T,
    )
    return updated.T, cluster_updated


def solution(mesh):
    split, whole = P(("px", "py"), None), P()
    return jax.shard_map(
        body,
        mesh=mesh,
        in_specs=(split,) * 4
        + (whole,) * 6
        + (split, P(("px", "py")))
        + (split,) * 3
        + (whole,) * 6,
        out_specs=(split, split),
        check_vma=False,
    )
```

```python
import jax
import jax.numpy as jnp
from jax import lax
from jax.experimental import pallas as pl
from jax.experimental.pallas import tpu as pltpu
from jax.sharding import PartitionSpec as P

WIDTH = 192
CLUST_DEV = 64
OWNERS = 16
BLOCK = 1024
F32, BF16, I32, I16 = jnp.float32, jnp.bfloat16, jnp.int32, jnp.int16


def nn(a, b):
    return jnp.dot(a, b, preferred_element_type=F32)


def nt(a, b):
    return lax.dot_general(a, b, (((1,), (1,)), ((), ())), preferred_element_type=F32)


def one_hot_rows(ids, count):
    row = lax.broadcasted_iota(I32, (count, ids.shape[1]), 0).astype(I16)
    return jnp.where(row == ids.astype(I16), jnp.ones_like(row, BF16), jnp.zeros_like(row, BF16))


def one_hot_lanes(ids, count):
    shape = (ids.shape[0], count)
    lane = lax.broadcasted_iota(I32, shape, 1).astype(I16)
    wide = jnp.broadcast_to(ids, (ids.shape[0], 128)).astype(I16)
    found = lane == jnp.tile(wide, (1, count // 128))
    return jnp.where(found, jnp.ones_like(lane, BF16), jnp.zeros_like(lane, BF16))


def half_silu(half):
    return half * jnp.tanh(half) + half


def normed(values, axis):
    center = values - jnp.mean(values, axis=axis, keepdims=True)
    return center * lax.rsqrt(jnp.mean(center * center, axis=axis, keepdims=True) + 1e-05)


def column(row, count):
    shape = (count, count)
    at = lax.broadcasted_iota(I32, shape, 0) == lax.broadcasted_iota(I32, shape, 1)
    return jnp.sum(jnp.where(at, row, 0.0), axis=1, keepdims=True)


def chooser(send, total):
    count = send.shape[1]
    ids = column(send.astype(F32), count).astype(I32)
    lane = lax.broadcasted_iota(I32, (count, total), 1)
    return jnp.where(lane == ids, 1.0, 0.0).astype(BF16)


def inside_flags():
    i, j = lax.axis_index("px"), lax.axis_index("py")
    return (i > 0, i < lax.axis_size("px") - 1, j > 0, j < lax.axis_size("py") - 1)


def halo_rows(refs):
    rows = []
    for ref, inside in zip(refs, inside_flags()):
        rows.append(jnp.where(inside, ref[...].astype(F32), 0.0).astype(BF16))
    return jnp.concatenate(rows, axis=0)


def pick_kernel(*refs):
    count = (len(refs) - 2) // 2
    sources, out_ref, targets, sems = refs[:count], refs[count], refs[count + 1 : -1], refs[-1]
    copies = fetch(sources, targets, sems)
    copies[0].wait()
    copies[1].wait()
    send_ref, table_ref = targets[:2]
    chosen = chooser(send_ref[...], table_ref.shape[1])
    out_ref[...] = nt(chosen, table_ref[...]).astype(BF16)
    for copy in copies[2:]:
        copy.wait()


def prepare_kernel(
    send3_ref,
    bias_ref,
    nbias_ref,
    wout_ref,
    nout_ref,
    feat_ref,
    win_ref,
    own_ref,
    into_ref,
    cols_ref,
    wide_ref,
    chosen_ref,
):
    chosen_ref[...] = chooser(send3_ref[...], CLUST_DEV)
    features = feat_ref[...]
    own_ref[...] = (0.5 * nn(win_ref[:, :WIDTH], features)).astype(BF16)
    into_ref[...] = (0.5 * nn(win_ref[:, WIDTH:], features)).astype(BF16)
    wide_ref[0] = wout_ref[...].astype(F32).T.astype(BF16)
    wide_ref[1] = nout_ref[...].astype(F32).T.astype(BF16)
    cols_ref[0] = jnp.broadcast_to(column(0.5 * bias_ref[...], WIDTH), (WIDTH, 128))
    cols_ref[1] = jnp.broadcast_to(column(0.5 * nbias_ref[...], WIDTH), (WIDTH, 128))


def fine_kernel(*refs):
    far = (len(refs) - 22) // 2
    sources, near, refs = refs[:far], refs[far : far + 15], refs[far + 15 :]
    (updated_ref, payload_ref), targets, refs = refs[:2], refs[2 : 2 + far], refs[2 + far :]
    picks_ref, totals_ref, result_ref, sems, result_sem = refs
    copies = fetch(sources, targets, sems)
    leave = pltpu.make_async_copy(result_ref, updated_ref, result_sem)
    fine_round(*near, result_ref, leave, payload_ref, picks_ref, totals_ref)
    for copy in copies:
        copy.wait()
    leave.wait()


def fine_round(
    feat_ref,
    own_ref,
    into_ref,
    cols_ref,
    wide_ref,
    h0,
    h1,
    h2,
    h3,
    src_ref,
    tgt_ref,
    win_ref,
    nin_ref,
    owner_ref,
    member_ref,
    updated_ref,
    leave,
    payload_ref,
    picks_ref,
    totals_ref,
):
    nodes = feat_ref.shape[1]
    rim = halo_rows((h0, h1, h2, h3))
    lookups = nodes + rim.shape[0]
    picks_ref[:, :nodes] = own_ref[...]
    picks_ref[:, nodes:lookups] = (0.5 * nt(win_ref[:, :WIDTH], rim)).astype(BF16)
    picks_ref[:, lookups:] = into_ref[...]
    for step in range(src_ref.shape[1] // BLOCK):
        at = pl.ds(step * BLOCK, BLOCK)
        from_source = one_hot_rows(src_ref[:, at], lookups)
        to_target = one_hot_rows(tgt_ref[:, at], nodes)
        half = nn(picks_ref[...], jnp.concatenate([from_source, to_target], axis=0))
        hidden = half_silu(half + jnp.tile(cols_ref[0], (1, BLOCK // 128))).astype(BF16)
        message = normed(nn(wide_ref[0], hidden), 0).astype(BF16)
        added = nt(message, to_target)
        if step == 0:
            totals_ref[...] = added
        else:
            totals_ref[...] += added

    features = feat_ref[...]
    joined = jnp.concatenate([features, totals_ref[...].astype(BF16)], axis=0)
    half = 0.5 * nn(nin_ref[...], joined) + jnp.tile(cols_ref[1], (1, nodes // 128))
    updated = features.astype(F32) + normed(nn(wide_ref[1], half_silu(half).astype(BF16)), 0)
    updated = updated.astype(BF16)
    updated_ref[...] = updated
    leave.start()

    position = owner_ref[...] * CLUST_DEV + member_ref[...]
    counted = jnp.concatenate([updated, jnp.ones((16, nodes), BF16)], axis=0)
    member_of = one_hot_rows(position, OWNERS * CLUST_DEV)
    pooled = nt(counted, member_of)
    for pair in range(OWNERS // 2):
        part = pooled[:, pair * 2 * CLUST_DEV : (pair + 1) * 2 * CLUST_DEV]
        half = WIDTH // 2
        top, low, count = part[:half], part[half:WIDTH], part[WIDTH : WIDTH + 8]
        left = lax.broadcasted_iota(I32, (half, 2 * CLUST_DEV), 1) < CLUST_DEV
        payload_ref[2 * pair, :half, :] = jnp.where(
            left, top, pltpu.roll(low, CLUST_DEV, 1)
        ).astype(BF16)
        payload_ref[2 * pair, half:, :] = count.astype(BF16)
        payload_ref[2 * pair + 1, :half, :] = jnp.where(
            left, pltpu.roll(top, CLUST_DEV, 1), low
        ).astype(BF16)
        payload_ref[2 * pair + 1, half:, :] = pltpu.roll(count, CLUST_DEV, 1).astype(BF16)


def coarse_kernel(parts_ref, chosen_ref, coarse_ref, shared_ref):
    total = jnp.sum(parts_ref[...].astype(F32), axis=0)
    half = WIDTH // 2
    sums = jnp.concatenate([total[:half], pltpu.roll(total[:half], CLUST_DEV, 1)], axis=0)
    counts = total[half : half + 1]
    coarse = (sums / jnp.maximum(counts, 1.0)).astype(BF16)[:, :CLUST_DEV]
    coarse_ref[...] = coarse
    shared_ref[...] = nt(chosen_ref[...], coarse).astype(BF16)


def prepare3_kernel(
    src_ref,
    tgt_ref,
    bias_ref,
    nbias_ref,
    wout_ref,
    nout_ref,
    feat_ref,
    win_ref,
    half_ref,
    around_ref,
    target_ref,
    cols_ref,
    wide_ref,
):
    features = feat_ref[...]
    nodes = features.shape[1]
    own = (0.5 * nn(win_ref[:, :WIDTH], features)).astype(BF16)
    into = (0.5 * nn(win_ref[:, WIDTH:], features)).astype(BF16)
    from_own = one_hot_rows(src_ref[...], nodes)
    to_target = one_hot_rows(tgt_ref[...], nodes)
    target_ref[...] = to_target
    around_ref[...] = one_hot_rows(src_ref[...] - nodes, around_ref.shape[0])
    half_ref[...] = nn(own, from_own) + nn(into, to_target) + column(0.5 * bias_ref[...], WIDTH)
    wide_ref[0] = wout_ref[...].astype(F32).T.astype(BF16)
    wide_ref[1] = nout_ref[...].astype(F32).T.astype(BF16)
    cols_ref[...] = jnp.broadcast_to(column(0.5 * nbias_ref[...], WIDTH), (WIDTH, nodes))


def level3_kernel(
    feat_ref,
    half_ref,
    around_ref,
    target_ref,
    cols_ref,
    wide_ref,
    h0,
    h1,
    h2,
    h3,
    win_ref,
    nin_ref,
    updated_ref,
):
    features = feat_ref[...]
    nodes = features.shape[1]
    rim = halo_rows((h0, h1, h2, h3))
    near = (0.5 * nt(win_ref[:, :WIDTH], rim)).astype(BF16)
    hidden = half_silu(half_ref[...] + nn(near, around_ref[...])).astype(BF16)
    message = normed(nn(wide_ref[0], hidden), 0).astype(BF16)
    totals = nt(message, target_ref[...])
    joined = jnp.concatenate([features, totals.astype(BF16)], axis=0)
    hidden = half_silu(0.5 * nn(nin_ref[...], joined) + cols_ref[...]).astype(BF16)
    updated = features.astype(F32) + normed(nn(wide_ref[1], hidden), 0)
    wide = jnp.concatenate([updated, jnp.zeros_like(updated)], axis=1)
    updated_ref[...] = wide.T[:nodes].astype(BF16)


def exchange(shared):
    found = []
    for axis, closed in (("px", False), ("py", True)):
        count = lax.axis_size(axis)
        ahead = [(k, (k + 1) % count) for k in range(count if closed else count - 1)]
        found.append(lax.ppermute(shared, axis, ahead))
        found.append(lax.ppermute(shared, axis, [(b, a) for a, b in ahead]))
    return found


def fetch(sources, targets, sems):
    copies = [
        pltpu.make_async_copy(source, target, sems.at[k])
        for k, (source, target) in enumerate(zip(sources, targets))
    ]
    for copy in copies:
        copy.start()
    return copies


def call(kernel, outs, scratch, *args, far=(), leave=()):
    held, away = pl.BlockSpec(memory_space=pltpu.VMEM), pl.BlockSpec(memory_space=pl.ANY)
    return pl.pallas_call(
        kernel,
        out_shape=[
            (jax.ShapeDtypeStruct if k in leave else pltpu.VMEM)(*out) for k, out in enumerate(outs)
        ],
        in_specs=[away] * len(far) + [held] * len(args),
        out_specs=[away if far and k in leave else held for k in range(len(outs))],
        scratch_shapes=scratch,
        name=kernel.__name__,
    )(*far, *[pltpu.with_memory_space_constraint(arg, pltpu.VMEM) for arg in args])


def body(
    node_features,
    edge_source,
    edge_target,
    halo_send,
    edge_weight_in,
    edge_bias,
    edge_weight_out,
    node_weight_in,
    node_bias,
    node_weight_out,
    cluster_owner,
    cluster_member,
    coarse_send,
    coarse_source,
    coarse_target,
    coarse_edge_in,
    coarse_edge_bias,
    coarse_edge_out,
    coarse_node_in,
    coarse_node_bias,
    coarse_node_out,
):
    nodes = node_features.shape[0]
    outs = lambda arrays: [(array.shape, array.dtype) for array in arrays]
    dma = pltpu.SemaphoreType.DMA
    held = (
        halo_send,
        node_features.T,
        coarse_send,
        edge_bias[None],
        node_bias[None],
        edge_weight_out,
        node_weight_out,
        edge_weight_in.T,
        node_weight_in.T,
        edge_source,
        edge_target,
        cluster_owner.reshape(1, nodes),
        cluster_member.reshape(1, nodes),
    )
    shared, _, features, send3, bias, nbias, w_out, n_out, w_in, n_in, *ids = call(
        pick_kernel,
        [((halo_send.shape[1], WIDTH), BF16)] + outs(held),
        [dma((len(held),))],
        far=held,
    )
    rims = exchange(shared)
    own, into, cols, wide, chosen = call(
        prepare_kernel,
        [
            ((WIDTH, nodes), BF16),
            ((WIDTH, nodes), BF16),
            ((2, WIDTH, 128), F32),
            ((2, WIDTH, WIDTH), BF16),
            ((coarse_send.shape[1], CLUST_DEV), BF16),
        ],
        [],
        send3,
        bias,
        nbias,
        w_out,
        n_out,
        features,
        w_in,
    )
    source, target, owner, member = ids
    far3 = (
        coarse_source,
        coarse_target,
        coarse_edge_bias[None],
        coarse_node_bias[None],
        coarse_edge_out,
        coarse_node_out,
        coarse_edge_in.T,
        coarse_node_in.T,
    )
    updated, payload, *held3 = call(
        fine_kernel,
        [((WIDTH, nodes), BF16), ((OWNERS, WIDTH // 2 + 8, 2 * CLUST_DEV), BF16)] + outs(far3),
        [
            pltpu.VMEM((WIDTH, 1280), BF16),
            pltpu.VMEM((WIDTH, nodes), F32),
            pltpu.VMEM((WIDTH, nodes), BF16),
            dma((len(far3),)),
            dma,
        ],
        features,
        own,
        into,
        cols,
        wide,
        *rims,
        source,
        target,
        w_in,
        n_in,
        owner,
        member,
        far=far3,
        leave=(0,),
    )
    w_in3, n_in3 = held3[6:]
    parts = lax.all_to_all(payload, "py", 0, 0, tiled=True)
    coarse, coarse_shared = call(
        coarse_kernel,
        [((WIDTH, CLUST_DEV), BF16), ((coarse_send.shape[1], WIDTH), BF16)],
        [],
        parts,
        chosen,
    )
    coarse_rims = exchange(coarse_shared)
    links = coarse_source.shape[1]
    prepared = call(
        prepare3_kernel,
        [
            ((WIDTH, links), F32),
            ((4 * coarse_send.shape[1], links), BF16),
            ((CLUST_DEV, links), BF16),
            ((WIDTH, CLUST_DEV), F32),
            ((2, WIDTH, WIDTH), BF16),
        ],
        [],
        *held3[:6],
        coarse,
        w_in3,
    )
    (cluster_updated,) = call(
        level3_kernel,
        [((CLUST_DEV, WIDTH), BF16)],
        [],
        coarse,
        *prepared,
        *coarse_rims,
        w_in3,
        n_in3,
        leave=(0,),
    )
    return updated.T, cluster_updated


def solution(mesh):
    split, whole = P(("px", "py"), None), P()
    return jax.shard_map(
        body,
        mesh=mesh,
        in_specs=(split,) * 4
        + (whole,) * 6
        + (split, P(("px", "py")))
        + (split,) * 3
        + (whole,) * 6,
        out_specs=(split, split),
        check_vma=False,
    )
```

```python
import jax
import jax.numpy as jnp
from jax import lax
from jax.experimental import pallas as pl
from jax.experimental.pallas import tpu as pltpu
from jax.sharding import PartitionSpec as P

WIDTH = 192
CLUST_DEV = 64
OWNERS = 16
BLOCK = 1024
F32, BF16, I32, I16 = jnp.float32, jnp.bfloat16, jnp.int32, jnp.int16


def nn(a, b):
    return jnp.dot(a, b, preferred_element_type=F32)


def nt(a, b):
    return lax.dot_general(a, b, (((1,), (1,)), ((), ())), preferred_element_type=F32)


def one_hot_rows(ids, count):
    row = lax.broadcasted_iota(I32, (count, ids.shape[1]), 0).astype(I16)
    return jnp.where(row == ids.astype(I16), jnp.ones_like(row, BF16), jnp.zeros_like(row, BF16))


def one_hot_lanes(ids, count):
    shape = (ids.shape[0], count)
    lane = lax.broadcasted_iota(I32, shape, 1).astype(I16)
    wide = jnp.broadcast_to(ids, (ids.shape[0], 128)).astype(I16)
    found = lane == jnp.tile(wide, (1, count // 128))
    return jnp.where(found, jnp.ones_like(lane, BF16), jnp.zeros_like(lane, BF16))


def half_silu(half):
    return half * jnp.tanh(half) + half


def normed(values, axis):
    center = values - jnp.mean(values, axis=axis, keepdims=True)
    return center * lax.rsqrt(jnp.mean(center * center, axis=axis, keepdims=True) + 1e-05)


def column(row, count):
    shape = (count, count)
    at = lax.broadcasted_iota(I32, shape, 0) == lax.broadcasted_iota(I32, shape, 1)
    return jnp.sum(jnp.where(at, row, 0.0), axis=1, keepdims=True)


def chooser(send, total):
    count = send.shape[1]
    ids = column(send.astype(F32), count).astype(I32)
    lane = lax.broadcasted_iota(I32, (count, total), 1)
    return jnp.where(lane == ids, 1.0, 0.0).astype(BF16)


def halo_rows(refs):
    i, j = lax.axis_index("px"), lax.axis_index("py")
    even, odd, low, high = [ref[...].astype(F32) for ref in refs]
    is_odd = lax.rem(i, 2) == 1
    inside = (i > 0, i < lax.axis_size("px") - 1, j > 0, j < lax.axis_size("py") - 1)
    found = (jnp.where(is_odd, even, odd), jnp.where(is_odd, odd, even), low, high)
    rows = [jnp.where(flag, part, 0.0).astype(BF16) for flag, part in zip(inside, found)]
    return jnp.concatenate(rows, axis=0)


def pick_kernel(*refs):
    count = (len(refs) - 2) // 2
    sources, out_ref, targets, sems = refs[:count], refs[count], refs[count + 1 : -1], refs[-1]
    copies = fetch(sources, targets, sems)
    copies[0].wait()
    copies[1].wait()
    send_ref, table_ref = targets[:2]
    chosen = chooser(send_ref[...], table_ref.shape[1])
    out_ref[...] = nt(chosen, table_ref[...]).astype(BF16)
    for copy in copies[2:]:
        copy.wait()


def prepare_kernel(*refs):
    count = (len(refs) - 7) // 2
    sources, feat_ref = refs[:count], refs[count]
    own_ref, into_ref, cols_ref, wide_ref, chosen_ref = refs[count + 1 : count + 6]
    targets, sems = refs[count + 6 : -1], refs[-1]
    copies = fetch(sources, targets, sems)
    win_ref, send3_ref, bias_ref, nbias_ref, wout_ref, nout_ref = targets[:6]
    for copy in copies[:6]:
        copy.wait()
    features = feat_ref[...]
    own_ref[...] = (0.5 * nn(win_ref[:, :WIDTH], features)).astype(BF16)
    into_ref[...] = (0.5 * nn(win_ref[:, WIDTH:], features)).astype(BF16)
    wide_ref[0] = wout_ref[...].astype(F32).T.astype(BF16)
    wide_ref[1] = nout_ref[...].astype(F32).T.astype(BF16)
    cols_ref[0] = jnp.broadcast_to(column(0.5 * bias_ref[...], WIDTH), (WIDTH, 128))
    cols_ref[1] = jnp.broadcast_to(column(0.5 * nbias_ref[...], WIDTH), (WIDTH, 128))
    chosen_ref[...] = chooser(send3_ref[...], CLUST_DEV)
    for copy in copies[6:]:
        copy.wait()


def fine_kernel(
    feat_ref,
    own_ref,
    into_ref,
    cols_ref,
    wide_ref,
    h0,
    h1,
    h2,
    h3,
    src_ref,
    tgt_ref,
    win_ref,
    nin_ref,
    owner_ref,
    member_ref,
    updated_ref,
    payload_ref,
    picks_ref,
    totals_ref,
):
    nodes = feat_ref.shape[1]
    rim = halo_rows((h0, h1, h2, h3))
    lookups = nodes + rim.shape[0]
    picks_ref[:, :nodes] = own_ref[...]
    picks_ref[:, nodes:lookups] = (0.5 * nt(win_ref[:, :WIDTH], rim)).astype(BF16)
    picks_ref[:, lookups:] = into_ref[...]
    for step in range(src_ref.shape[1] // BLOCK):
        at = pl.ds(step * BLOCK, BLOCK)
        from_source = one_hot_rows(src_ref[:, at], lookups)
        to_target = one_hot_rows(tgt_ref[:, at], nodes)
        half = nn(picks_ref[...], jnp.concatenate([from_source, to_target], axis=0))
        hidden = half_silu(half + jnp.tile(cols_ref[0], (1, BLOCK // 128))).astype(BF16)
        message = normed(nn(wide_ref[0], hidden), 0).astype(BF16)
        added = nt(message, to_target)
        if step == 0:
            totals_ref[...] = added
        else:
            totals_ref[...] += added

    features = feat_ref[...]
    joined = jnp.concatenate([features, totals_ref[...].astype(BF16)], axis=0)
    half = 0.5 * nn(nin_ref[...], joined) + jnp.tile(cols_ref[1], (1, nodes // 128))
    updated = features.astype(F32) + normed(nn(wide_ref[1], half_silu(half).astype(BF16)), 0)
    updated = updated.astype(BF16)
    updated_ref[...] = updated

    position = owner_ref[...] * CLUST_DEV + member_ref[...]
    counted = jnp.concatenate([updated, jnp.ones((16, nodes), BF16)], axis=0)
    member_of = one_hot_rows(position, OWNERS * CLUST_DEV)
    pooled = nt(counted, member_of)
    for pair in range(OWNERS // 2):
        part = pooled[:, pair * 2 * CLUST_DEV : (pair + 1) * 2 * CLUST_DEV]
        half = WIDTH // 2
        top, low, count = part[:half], part[half:WIDTH], part[WIDTH : WIDTH + 8]
        left = lax.broadcasted_iota(I32, (half, 2 * CLUST_DEV), 1) < CLUST_DEV
        payload_ref[2 * pair, :half, :] = jnp.where(
            left, top, pltpu.roll(low, CLUST_DEV, 1)
        ).astype(BF16)
        payload_ref[2 * pair, half:, :] = count.astype(BF16)
        payload_ref[2 * pair + 1, :half, :] = jnp.where(
            left, pltpu.roll(top, CLUST_DEV, 1), low
        ).astype(BF16)
        payload_ref[2 * pair + 1, half:, :] = pltpu.roll(count, CLUST_DEV, 1).astype(BF16)


def coarse_kernel(parts_ref, chosen_ref, coarse_ref, shared_ref):
    total = jnp.sum(parts_ref[...].astype(F32), axis=0)
    half = WIDTH // 2
    sums = jnp.concatenate([total[:half], pltpu.roll(total[:half], CLUST_DEV, 1)], axis=0)
    counts = total[half : half + 1]
    coarse = (sums / jnp.maximum(counts, 1.0)).astype(BF16)[:, :CLUST_DEV]
    coarse_ref[...] = coarse
    shared_ref[...] = nt(chosen_ref[...], coarse).astype(BF16)


def prepare3_kernel(
    src_ref,
    tgt_ref,
    bias_ref,
    nbias_ref,
    wout_ref,
    nout_ref,
    feat_ref,
    win_ref,
    half_ref,
    around_ref,
    target_ref,
    cols_ref,
    wide_ref,
):
    features = feat_ref[...]
    nodes = features.shape[1]
    own = (0.5 * nn(win_ref[:, :WIDTH], features)).astype(BF16)
    into = (0.5 * nn(win_ref[:, WIDTH:], features)).astype(BF16)
    from_own = one_hot_rows(src_ref[...], nodes)
    to_target = one_hot_rows(tgt_ref[...], nodes)
    target_ref[...] = to_target
    around_ref[...] = one_hot_rows(src_ref[...] - nodes, around_ref.shape[0])
    half_ref[...] = nn(own, from_own) + nn(into, to_target) + column(0.5 * bias_ref[...], WIDTH)
    wide_ref[0] = wout_ref[...].astype(F32).T.astype(BF16)
    wide_ref[1] = nout_ref[...].astype(F32).T.astype(BF16)
    cols_ref[...] = jnp.broadcast_to(column(0.5 * nbias_ref[...], WIDTH), (WIDTH, nodes))


def level3_kernel(
    feat_ref,
    half_ref,
    around_ref,
    target_ref,
    cols_ref,
    wide_ref,
    h0,
    h1,
    h2,
    h3,
    win_ref,
    nin_ref,
    updated_ref,
):
    features = feat_ref[...]
    nodes = features.shape[1]
    rim = halo_rows((h0, h1, h2, h3))
    near = (0.5 * nt(win_ref[:, :WIDTH], rim)).astype(BF16)
    hidden = half_silu(half_ref[...] + nn(near, around_ref[...])).astype(BF16)
    message = normed(nn(wide_ref[0], hidden), 0).astype(BF16)
    totals = nt(message, target_ref[...])
    joined = jnp.concatenate([features, totals.astype(BF16)], axis=0)
    hidden = half_silu(0.5 * nn(nin_ref[...], joined) + cols_ref[...]).astype(BF16)
    updated = features.astype(F32) + normed(nn(wide_ref[1], hidden), 0)
    wide = jnp.concatenate([updated, jnp.zeros_like(updated)], axis=1)
    updated_ref[...] = wide.T[:nodes].astype(BF16)


def exchange(shared):
    count = lax.axis_size("py")
    ahead = [(k, (k + 1) % count) for k in range(count)]
    along = [lax.ppermute(shared, "py", ahead)]
    along.append(lax.ppermute(shared, "py", [(b, a) for a, b in ahead]))
    across = []
    for first in (0, 1):
        pairs = [(k, k + 1) for k in range(first, lax.axis_size("px") - 1, 2)]
        across.append(lax.ppermute(shared, "px", pairs + [(b, a) for a, b in pairs]))
    return across + along


def fetch(sources, targets, sems):
    copies = [
        pltpu.make_async_copy(source, target, sems.at[k])
        for k, (source, target) in enumerate(zip(sources, targets))
    ]
    for copy in copies:
        copy.start()
    return copies


def call(kernel, outs, scratch, *args, far=(), leave=()):
    held, away = pl.BlockSpec(memory_space=pltpu.VMEM), pl.BlockSpec(memory_space=pl.ANY)
    return pl.pallas_call(
        kernel,
        out_shape=[
            (jax.ShapeDtypeStruct if k in leave else pltpu.VMEM)(*out) for k, out in enumerate(outs)
        ],
        in_specs=[away] * len(far) + [held] * len(args),
        out_specs=[away if far and k in leave else held for k in range(len(outs))],
        scratch_shapes=scratch,
        name=kernel.__name__,
    )(*far, *[pltpu.with_memory_space_constraint(arg, pltpu.VMEM) for arg in args])


def body(
    node_features,
    edge_source,
    edge_target,
    halo_send,
    edge_weight_in,
    edge_bias,
    edge_weight_out,
    node_weight_in,
    node_bias,
    node_weight_out,
    cluster_owner,
    cluster_member,
    coarse_send,
    coarse_source,
    coarse_target,
    coarse_edge_in,
    coarse_edge_bias,
    coarse_edge_out,
    coarse_node_in,
    coarse_node_bias,
    coarse_node_out,
):
    nodes = node_features.shape[0]
    outs = lambda arrays: [(array.shape, array.dtype) for array in arrays]
    dma = pltpu.SemaphoreType.DMA
    held = (halo_send, node_features.T)
    shared, _, features = call(
        pick_kernel,
        [((halo_send.shape[1], WIDTH), BF16)] + outs(held),
        [dma((len(held),))],
        far=held,
    )
    rims = exchange(shared)
    held = (
        edge_weight_in.T,
        coarse_send,
        edge_bias[None],
        node_bias[None],
        edge_weight_out,
        node_weight_out,
        node_weight_in.T,
        edge_source,
        edge_target,
        cluster_owner.reshape(1, nodes),
        cluster_member.reshape(1, nodes),
        coarse_source,
        coarse_target,
        coarse_edge_bias[None],
        coarse_node_bias[None],
    )
    own, into, cols, wide, chosen, *held = call(
        prepare_kernel,
        [
            ((WIDTH, nodes), BF16),
            ((WIDTH, nodes), BF16),
            ((2, WIDTH, 128), F32),
            ((2, WIDTH, WIDTH), BF16),
            ((coarse_send.shape[1], CLUST_DEV), BF16),
        ]
        + outs(held),
        [dma((len(held),))],
        features,
        far=held,
    )
    w_in, n_in, source, target, owner, member = held[:1] + held[6:11]
    updated, payload = call(
        fine_kernel,
        [((WIDTH, nodes), BF16), ((OWNERS, WIDTH // 2 + 8, 2 * CLUST_DEV), BF16)],
        [pltpu.VMEM((WIDTH, 1280), BF16), pltpu.VMEM((WIDTH, nodes), F32)],
        features,
        own,
        into,
        cols,
        wide,
        *rims,
        source,
        target,
        w_in,
        n_in,
        owner,
        member,
        leave=(0,),
    )
    parts = lax.all_to_all(payload, "py", 0, 0, tiled=True)
    coarse, coarse_shared = call(
        coarse_kernel,
        [((WIDTH, CLUST_DEV), BF16), ((coarse_send.shape[1], WIDTH), BF16)],
        [],
        parts,
        chosen,
    )
    coarse_rims = exchange(coarse_shared)
    links = coarse_source.shape[1]
    prepared = call(
        prepare3_kernel,
        [
            ((WIDTH, links), F32),
            ((4 * coarse_send.shape[1], links), BF16),
            ((CLUST_DEV, links), BF16),
            ((WIDTH, CLUST_DEV), F32),
            ((2, WIDTH, WIDTH), BF16),
        ],
        [],
        *held[11:],
        coarse_edge_out,
        coarse_node_out,
        coarse,
        coarse_edge_in.T,
    )
    (cluster_updated,) = call(
        level3_kernel,
        [((CLUST_DEV, WIDTH), BF16)],
        [],
        coarse,
        *prepared,
        *coarse_rims,
        coarse_edge_in.T,
        coarse_node_in.T,
        leave=(0,),
    )
    return updated.T, cluster_updated


def solution(mesh):
    split, whole = P(("px", "py"), None), P()
    return jax.shard_map(
        body,
        mesh=mesh,
        in_specs=(split,) * 4
        + (whole,) * 6
        + (split, P(("px", "py")))
        + (split,) * 3
        + (whole,) * 6,
        out_specs=(split, split),
        check_vma=False,
    )
```

```python
import jax
import jax.numpy as jnp
from jax import lax
from jax.experimental import pallas as pl
from jax.experimental.pallas import tpu as pltpu
from jax.sharding import PartitionSpec as P

WIDTH = 192
CLUST_DEV = 64
OWNERS = 16
BLOCK, AHEAD = 1024, 3
F32, BF16, I32, I16 = jnp.float32, jnp.bfloat16, jnp.int32, jnp.int16


def nn(a, b):
    return jnp.dot(a, b, preferred_element_type=F32)


def nt(a, b):
    return lax.dot_general(a, b, (((1,), (1,)), ((), ())), preferred_element_type=F32)


def one_hot_rows(ids, count):
    row = lax.broadcasted_iota(I32, (count, ids.shape[1]), 0).astype(I16)
    return jnp.where(row == ids.astype(I16), jnp.ones_like(row, BF16), jnp.zeros_like(row, BF16))


def one_hot_lanes(ids, count):
    shape = (ids.shape[0], count)
    lane = lax.broadcasted_iota(I32, shape, 1).astype(I16)
    wide = jnp.broadcast_to(ids, (ids.shape[0], 128)).astype(I16)
    found = lane == jnp.tile(wide, (1, count // 128))
    return jnp.where(found, jnp.ones_like(lane, BF16), jnp.zeros_like(lane, BF16))


def half_silu(half):
    return half * jnp.tanh(half) + half


def normed(values, axis):
    center = values - jnp.mean(values, axis=axis, keepdims=True)
    return center * lax.rsqrt(jnp.mean(center * center, axis=axis, keepdims=True) + 1e-05)


def column(row, count):
    shape = (count, count)
    at = lax.broadcasted_iota(I32, shape, 0) == lax.broadcasted_iota(I32, shape, 1)
    return jnp.sum(jnp.where(at, row, 0.0), axis=1, keepdims=True)


def chooser(send, total):
    count = send.shape[1]
    ids = column(send.astype(F32), count).astype(I32)
    lane = lax.broadcasted_iota(I32, (count, total), 1)
    return jnp.where(lane == ids, 1.0, 0.0).astype(BF16)


def halo_rows(refs):
    i, j = lax.axis_index("px"), lax.axis_index("py")
    even, odd, low, high = [ref[...].astype(F32) for ref in refs]
    is_odd = lax.rem(i, 2) == 1
    inside = (i > 0, i < lax.axis_size("px") - 1, j > 0, j < lax.axis_size("py") - 1)
    found = (jnp.where(is_odd, even, odd), jnp.where(is_odd, odd, even), low, high)
    rows = [jnp.where(flag, part, 0.0).astype(BF16) for flag, part in zip(inside, found)]
    return jnp.concatenate(rows, axis=0)


def pick_kernel(*refs):
    count = (len(refs) - 2) // 2
    sources, out_ref, targets, sems = refs[:count], refs[count], refs[count + 1 : -1], refs[-1]
    copies = fetch(sources, targets, sems)
    copies[0].wait()
    copies[1].wait()
    send_ref, table_ref = targets[:2]
    chosen = chooser(send_ref[...], table_ref.shape[1])
    out_ref[...] = nt(chosen, table_ref[...]).astype(BF16)
    for copy in copies[2:]:
        copy.wait()


def prepare_kernel(*refs):
    count = (len(refs) - 10) // 2
    sources, (feat_ref, win_ref, src_ref, tgt_ref) = refs[:count], refs[count : count + 4]
    picks_ref, cols_ref, wide_ref, chosen_ref, begun_ref = refs[count + 4 : count + 9]
    targets, sems = refs[count + 9 : -1], refs[-1]
    send3_ref, bias_ref, nbias_ref, wout_ref, nout_ref = targets[:5]
    copies = fetch(sources, targets, sems)
    features = feat_ref[...]
    nodes = features.shape[1]
    picks_ref[:, :nodes] = (0.5 * nn(win_ref[:, :WIDTH], features)).astype(BF16)
    picks_ref[:, nodes:] = (0.5 * nn(win_ref[:, WIDTH:], features)).astype(BF16)
    for step in range(AHEAD):
        at = pl.ds(step * BLOCK, BLOCK)
        from_own = one_hot_rows(src_ref[:, at], nodes)
        to_target = one_hot_rows(tgt_ref[:, at], nodes)
        begun_ref[:, at] = nn(picks_ref[...], jnp.concatenate([from_own, to_target], axis=0))
    for copy in copies:
        copy.wait()
    wide_ref[0] = wout_ref[...].astype(F32).T.astype(BF16)
    wide_ref[1] = nout_ref[...].astype(F32).T.astype(BF16)
    cols_ref[0] = jnp.broadcast_to(column(0.5 * bias_ref[...], WIDTH), (WIDTH, 128))
    cols_ref[1] = jnp.broadcast_to(column(0.5 * nbias_ref[...], WIDTH), (WIDTH, 128))
    chosen_ref[...] = chooser(send3_ref[...], CLUST_DEV)


def fine_kernel(
    feat_ref,
    made_ref,
    cols_ref,
    wide_ref,
    begun_ref,
    h0,
    h1,
    h2,
    h3,
    src_ref,
    tgt_ref,
    win_ref,
    nin_ref,
    owner_ref,
    member_ref,
    updated_ref,
    payload_ref,
    picks_ref,
    totals_ref,
):
    nodes = feat_ref.shape[1]
    rim = halo_rows((h0, h1, h2, h3))
    around = (0.5 * nt(win_ref[:, :WIDTH], rim)).astype(BF16)
    picks_ref[:, : 2 * nodes] = made_ref[...]
    picks_ref[:, 2 * nodes :] = around
    for step in range(src_ref.shape[1] // BLOCK):
        at = pl.ds(step * BLOCK, BLOCK)
        to_target = one_hot_rows(tgt_ref[:, at], nodes)
        from_rim = one_hot_rows(src_ref[:, at] - nodes, rim.shape[0])
        if step < AHEAD:
            half = begun_ref[:, at] + nn(around, from_rim)
        else:
            from_own = one_hot_rows(src_ref[:, at], nodes)
            chosen = jnp.concatenate([from_own, to_target, from_rim], axis=0)
            half = nn(picks_ref[...], chosen)
        hidden = half_silu(half + jnp.tile(cols_ref[0], (1, BLOCK // 128))).astype(BF16)
        message = normed(nn(wide_ref[0], hidden), 0).astype(BF16)
        added = nt(message, to_target)
        if step == 0:
            totals_ref[...] = added
        else:
            totals_ref[...] += added

    features = feat_ref[...]
    joined = jnp.concatenate([features, totals_ref[...].astype(BF16)], axis=0)
    half = 0.5 * nn(nin_ref[...], joined) + jnp.tile(cols_ref[1], (1, nodes // 128))
    updated = features.astype(F32) + normed(nn(wide_ref[1], half_silu(half).astype(BF16)), 0)
    updated = updated.astype(BF16)
    updated_ref[...] = updated

    position = owner_ref[...] * CLUST_DEV + member_ref[...]
    counted = jnp.concatenate([updated, jnp.ones((16, nodes), BF16)], axis=0)
    member_of = one_hot_rows(position, OWNERS * CLUST_DEV)
    pooled = nt(counted, member_of)
    for pair in range(OWNERS // 2):
        part = pooled[:, pair * 2 * CLUST_DEV : (pair + 1) * 2 * CLUST_DEV]
        half = WIDTH // 2
        top, low, count = part[:half], part[half:WIDTH], part[WIDTH : WIDTH + 8]
        left = lax.broadcasted_iota(I32, (half, 2 * CLUST_DEV), 1) < CLUST_DEV
        payload_ref[2 * pair, :half, :] = jnp.where(
            left, top, pltpu.roll(low, CLUST_DEV, 1)
        ).astype(BF16)
        payload_ref[2 * pair, half:, :] = count.astype(BF16)
        payload_ref[2 * pair + 1, :half, :] = jnp.where(
            left, pltpu.roll(top, CLUST_DEV, 1), low
        ).astype(BF16)
        payload_ref[2 * pair + 1, half:, :] = pltpu.roll(count, CLUST_DEV, 1).astype(BF16)


def coarse_kernel(parts_ref, chosen_ref, coarse_ref, shared_ref):
    total = jnp.sum(parts_ref[...].astype(F32), axis=0)
    half = WIDTH // 2
    sums = jnp.concatenate([total[:half], pltpu.roll(total[:half], CLUST_DEV, 1)], axis=0)
    counts = total[half : half + 1]
    coarse = (sums / jnp.maximum(counts, 1.0)).astype(BF16)[:, :CLUST_DEV]
    coarse_ref[...] = coarse
    shared_ref[...] = nt(chosen_ref[...], coarse).astype(BF16)


def prepare3_kernel(
    src_ref,
    tgt_ref,
    bias_ref,
    nbias_ref,
    wout_ref,
    nout_ref,
    feat_ref,
    win_ref,
    half_ref,
    around_ref,
    target_ref,
    cols_ref,
    wide_ref,
):
    features = feat_ref[...]
    nodes = features.shape[1]
    own = (0.5 * nn(win_ref[:, :WIDTH], features)).astype(BF16)
    into = (0.5 * nn(win_ref[:, WIDTH:], features)).astype(BF16)
    from_own = one_hot_rows(src_ref[...], nodes)
    to_target = one_hot_rows(tgt_ref[...], nodes)
    target_ref[...] = to_target
    around_ref[...] = one_hot_rows(src_ref[...] - nodes, around_ref.shape[0])
    half_ref[...] = nn(own, from_own) + nn(into, to_target) + column(0.5 * bias_ref[...], WIDTH)
    wide_ref[0] = wout_ref[...].astype(F32).T.astype(BF16)
    wide_ref[1] = nout_ref[...].astype(F32).T.astype(BF16)
    cols_ref[...] = jnp.broadcast_to(column(0.5 * nbias_ref[...], WIDTH), (WIDTH, nodes))


def level3_kernel(
    feat_ref,
    half_ref,
    around_ref,
    target_ref,
    cols_ref,
    wide_ref,
    h0,
    h1,
    h2,
    h3,
    win_ref,
    nin_ref,
    updated_ref,
):
    features = feat_ref[...]
    nodes = features.shape[1]
    rim = halo_rows((h0, h1, h2, h3))
    near = (0.5 * nt(win_ref[:, :WIDTH], rim)).astype(BF16)
    hidden = half_silu(half_ref[...] + nn(near, around_ref[...])).astype(BF16)
    message = normed(nn(wide_ref[0], hidden), 0).astype(BF16)
    totals = nt(message, target_ref[...])
    joined = jnp.concatenate([features, totals.astype(BF16)], axis=0)
    hidden = half_silu(0.5 * nn(nin_ref[...], joined) + cols_ref[...]).astype(BF16)
    updated = features.astype(F32) + normed(nn(wide_ref[1], hidden), 0)
    wide = jnp.concatenate([updated, jnp.zeros_like(updated)], axis=1)
    updated_ref[...] = wide.T[:nodes].astype(BF16)


def exchange(shared):
    count = lax.axis_size("py")
    ahead = [(k, (k + 1) % count) for k in range(count)]
    along = [lax.ppermute(shared, "py", ahead)]
    along.append(lax.ppermute(shared, "py", [(b, a) for a, b in ahead]))
    across = []
    for first in (0, 1):
        pairs = [(k, k + 1) for k in range(first, lax.axis_size("px") - 1, 2)]
        across.append(lax.ppermute(shared, "px", pairs + [(b, a) for a, b in pairs]))
    return across + along


def fetch(sources, targets, sems):
    copies = [
        pltpu.make_async_copy(source, target, sems.at[k])
        for k, (source, target) in enumerate(zip(sources, targets))
    ]
    for copy in copies:
        copy.start()
    return copies


def call(kernel, outs, scratch, *args, far=(), leave=()):
    held, away = pl.BlockSpec(memory_space=pltpu.VMEM), pl.BlockSpec(memory_space=pltpu.HBM)
    return pl.pallas_call(
        kernel,
        out_shape=[
            (jax.ShapeDtypeStruct if k in leave else pltpu.VMEM)(*out) for k, out in enumerate(outs)
        ],
        in_specs=[away] * len(far) + [held] * len(args),
        out_specs=[away if far and k in leave else held for k in range(len(outs))],
        scratch_shapes=scratch,
        compiler_params=pltpu.CompilerParams(vmem_limit_bytes=24 << 20),
        name=kernel.__name__,
    )(
        *[pltpu.with_memory_space_constraint(array, pltpu.HBM) for array in far],
        *[pltpu.with_memory_space_constraint(arg, pltpu.VMEM) for arg in args],
    )


def body(
    node_features,
    edge_source,
    edge_target,
    halo_send,
    edge_weight_in,
    edge_bias,
    edge_weight_out,
    node_weight_in,
    node_bias,
    node_weight_out,
    cluster_owner,
    cluster_member,
    coarse_send,
    coarse_source,
    coarse_target,
    coarse_edge_in,
    coarse_edge_bias,
    coarse_edge_out,
    coarse_node_in,
    coarse_node_bias,
    coarse_node_out,
):
    nodes = node_features.shape[0]
    outs = lambda arrays: [(array.shape, array.dtype) for array in arrays]
    dma = pltpu.SemaphoreType.DMA
    held = (halo_send, node_features.T, edge_weight_in.T, edge_source, edge_target)
    shared, _, features, w_in, source, target = call(
        pick_kernel,
        [((halo_send.shape[1], WIDTH), BF16)] + outs(held),
        [dma((len(held),))],
        far=held,
    )
    rims = exchange(shared)
    held = (
        coarse_send,
        edge_bias[None],
        node_bias[None],
        edge_weight_out,
        node_weight_out,
        node_weight_in.T,
        cluster_owner.reshape(1, nodes),
        cluster_member.reshape(1, nodes),
        coarse_source,
        coarse_target,
        coarse_edge_bias[None],
        coarse_node_bias[None],
    )
    picks, cols, wide, chosen, begun, *held = call(
        prepare_kernel,
        [
            ((WIDTH, 2 * nodes), BF16),
            ((2, WIDTH, 128), F32),
            ((2, WIDTH, WIDTH), BF16),
            ((coarse_send.shape[1], CLUST_DEV), BF16),
            ((WIDTH, AHEAD * BLOCK), F32),
        ]
        + outs(held),
        [dma((len(held),))],
        features,
        w_in,
        source,
        target,
        far=held,
    )
    n_in, owner, member = held[5:8]
    updated, payload = call(
        fine_kernel,
        [((WIDTH, nodes), BF16), ((OWNERS, WIDTH // 2 + 8, 2 * CLUST_DEV), BF16)],
        [pltpu.VMEM((WIDTH, 1280), BF16), pltpu.VMEM((WIDTH, nodes), F32)],
        features,
        picks,
        cols,
        wide,
        begun,
        *rims,
        source,
        target,
        w_in,
        n_in,
        owner,
        member,
        leave=(0,),
    )
    parts = lax.all_to_all(payload, "py", 0, 0, tiled=True)
    coarse, coarse_shared = call(
        coarse_kernel,
        [((WIDTH, CLUST_DEV), BF16), ((coarse_send.shape[1], WIDTH), BF16)],
        [],
        parts,
        chosen,
    )
    coarse_rims = exchange(coarse_shared)
    links = coarse_source.shape[1]
    prepared = call(
        prepare3_kernel,
        [
            ((WIDTH, links), F32),
            ((4 * coarse_send.shape[1], links), BF16),
            ((CLUST_DEV, links), BF16),
            ((WIDTH, CLUST_DEV), F32),
            ((2, WIDTH, WIDTH), BF16),
        ],
        [],
        *held[8:],
        coarse_edge_out,
        coarse_node_out,
        coarse,
        coarse_edge_in.T,
    )
    (cluster_updated,) = call(
        level3_kernel,
        [((CLUST_DEV, WIDTH), BF16)],
        [],
        coarse,
        *prepared,
        *coarse_rims,
        coarse_edge_in.T,
        coarse_node_in.T,
        leave=(0,),
    )
    return updated.T, cluster_updated


def solution(mesh):
    split, whole = P(("px", "py"), None), P()
    return jax.shard_map(
        body,
        mesh=mesh,
        in_specs=(split,) * 4
        + (whole,) * 6
        + (split, P(("px", "py")))
        + (split,) * 3
        + (whole,) * 6,
        out_specs=(split, split),
        check_vma=False,
    )
```

```python
import jax
import jax.numpy as jnp
from jax import lax
from jax.experimental import pallas as pl
from jax.experimental.pallas import tpu as pltpu
from jax.sharding import PartitionSpec as P

WIDTH = 192
CLUST_DEV = 64
OWNERS = 16
BLOCK = 1024
F32, BF16, I32, I16 = jnp.float32, jnp.bfloat16, jnp.int32, jnp.int16


def nn(a, b):
    return jnp.dot(a, b, preferred_element_type=F32)


def nt(a, b):
    return lax.dot_general(a, b, (((1,), (1,)), ((), ())), preferred_element_type=F32)


def one_hot_rows(ids, count):
    row = lax.broadcasted_iota(I32, (count, ids.shape[1]), 0).astype(I16)
    return jnp.where(row == ids.astype(I16), jnp.ones_like(row, BF16), jnp.zeros_like(row, BF16))


def one_hot_lanes(ids, count):
    shape = (ids.shape[0], count)
    lane = lax.broadcasted_iota(I32, shape, 1).astype(I16)
    wide = jnp.broadcast_to(ids, (ids.shape[0], 128)).astype(I16)
    found = lane == jnp.tile(wide, (1, count // 128))
    return jnp.where(found, jnp.ones_like(lane, BF16), jnp.zeros_like(lane, BF16))


def half_silu(half):
    return half * jnp.tanh(half) + half


def normed(values, axis):
    center = values - jnp.mean(values, axis=axis, keepdims=True)
    return center * lax.rsqrt(jnp.mean(center * center, axis=axis, keepdims=True) + 1e-05)


def column(row, count):
    shape = (count, count)
    at = lax.broadcasted_iota(I32, shape, 0) == lax.broadcasted_iota(I32, shape, 1)
    return jnp.sum(jnp.where(at, row, 0.0), axis=1, keepdims=True)


def chooser(send, total):
    count = send.shape[1]
    ids = column(send.astype(F32), count).astype(I32)
    lane = lax.broadcasted_iota(I32, (count, total), 1)
    return jnp.where(lane == ids, 1.0, 0.0).astype(BF16)


def halo_rows(refs):
    i, j = lax.axis_index("px"), lax.axis_index("py")
    even, odd, low, high = [ref[...].astype(F32) for ref in refs]
    is_odd = lax.rem(i, 2) == 1
    inside = (i > 0, i < lax.axis_size("px") - 1, j > 0, j < lax.axis_size("py") - 1)
    found = (jnp.where(is_odd, even, odd), jnp.where(is_odd, odd, even), low, high)
    rows = [jnp.where(flag, part, 0.0).astype(BF16) for flag, part in zip(inside, found)]
    return jnp.concatenate(rows, axis=0)


def pick_kernel(send_ref, table_ref, out_ref):
    out_ref[...] = nt(chooser(send_ref[...], table_ref.shape[1]), table_ref[...]).astype(BF16)


def prepare_kernel(*refs):
    count = (len(refs) - 7) // 2
    sources, feat_ref = refs[:count], refs[count]
    own_ref, into_ref, cols_ref, wide_ref, chosen_ref = refs[count + 1 : count + 6]
    targets, sems = refs[count + 6 : -1], refs[-1]
    copies = fetch(sources, targets, sems)
    win_ref, send3_ref, bias_ref, nbias_ref, wout_ref, nout_ref = targets[:6]
    for copy in copies[:6]:
        copy.wait()
    features = feat_ref[...]
    own_ref[...] = (0.5 * nn(win_ref[:, :WIDTH], features)).astype(BF16)
    into_ref[...] = (0.5 * nn(win_ref[:, WIDTH:], features)).astype(BF16)
    wide_ref[0] = wout_ref[...].astype(F32).T.astype(BF16)
    wide_ref[1] = nout_ref[...].astype(F32).T.astype(BF16)
    cols_ref[0] = jnp.broadcast_to(column(0.5 * bias_ref[...], WIDTH), (WIDTH, 128))
    cols_ref[1] = jnp.broadcast_to(column(0.5 * nbias_ref[...], WIDTH), (WIDTH, 128))
    chosen_ref[...] = chooser(send3_ref[...], CLUST_DEV)
    for copy in copies[6:]:
        copy.wait()


def fine_kernel(
    feat_ref,
    own_ref,
    into_ref,
    cols_ref,
    wide_ref,
    h0,
    h1,
    h2,
    h3,
    src_ref,
    tgt_ref,
    win_ref,
    nin_ref,
    owner_ref,
    member_ref,
    updated_ref,
    payload_ref,
    picks_ref,
    totals_ref,
):
    nodes = feat_ref.shape[1]
    rim = halo_rows((h0, h1, h2, h3))
    lookups = nodes + rim.shape[0]
    picks_ref[:, :nodes] = own_ref[...]
    picks_ref[:, nodes:lookups] = (0.5 * nt(win_ref[:, :WIDTH], rim)).astype(BF16)
    picks_ref[:, lookups:] = into_ref[...]
    for step in range(src_ref.shape[1] // BLOCK):
        at = pl.ds(step * BLOCK, BLOCK)
        from_source = one_hot_rows(src_ref[:, at], lookups)
        to_target = one_hot_rows(tgt_ref[:, at], nodes)
        half = nn(picks_ref[...], jnp.concatenate([from_source, to_target], axis=0))
        hidden = half_silu(half + jnp.tile(cols_ref[0], (1, BLOCK // 128))).astype(BF16)
        message = normed(nn(wide_ref[0], hidden), 0).astype(BF16)
        added = nt(message, to_target)
        if step == 0:
            totals_ref[...] = added
        else:
            totals_ref[...] += added

    features = feat_ref[...]
    joined = jnp.concatenate([features, totals_ref[...].astype(BF16)], axis=0)
    half = 0.5 * nn(nin_ref[...], joined) + jnp.tile(cols_ref[1], (1, nodes // 128))
    updated = features.astype(F32) + normed(nn(wide_ref[1], half_silu(half).astype(BF16)), 0)
    updated = updated.astype(BF16)
    updated_ref[...] = updated

    position = owner_ref[...] * CLUST_DEV + member_ref[...]
    counted = jnp.concatenate([updated, jnp.ones((16, nodes), BF16)], axis=0)
    member_of = one_hot_rows(position, OWNERS * CLUST_DEV)
    pooled = nt(counted, member_of)
    for pair in range(OWNERS // 2):
        part = pooled[:, pair * 2 * CLUST_DEV : (pair + 1) * 2 * CLUST_DEV]
        half = WIDTH // 2
        top, low, count = part[:half], part[half:WIDTH], part[WIDTH : WIDTH + 8]
        left = lax.broadcasted_iota(I32, (half, 2 * CLUST_DEV), 1) < CLUST_DEV
        payload_ref[2 * pair, :half, :] = jnp.where(
            left, top, pltpu.roll(low, CLUST_DEV, 1)
        ).astype(BF16)
        payload_ref[2 * pair, half:, :] = count.astype(BF16)
        payload_ref[2 * pair + 1, :half, :] = jnp.where(
            left, pltpu.roll(top, CLUST_DEV, 1), low
        ).astype(BF16)
        payload_ref[2 * pair + 1, half:, :] = pltpu.roll(count, CLUST_DEV, 1).astype(BF16)


def coarse_kernel(parts_ref, chosen_ref, coarse_ref, shared_ref):
    total = jnp.sum(parts_ref[...].astype(F32), axis=0)
    half = WIDTH // 2
    sums = jnp.concatenate([total[:half], pltpu.roll(total[:half], CLUST_DEV, 1)], axis=0)
    counts = total[half : half + 1]
    coarse = (sums / jnp.maximum(counts, 1.0)).astype(BF16)[:, :CLUST_DEV]
    coarse_ref[...] = coarse
    shared_ref[...] = nt(chosen_ref[...], coarse).astype(BF16)


def prepare3_kernel(
    src_ref,
    tgt_ref,
    bias_ref,
    nbias_ref,
    wout_ref,
    nout_ref,
    feat_ref,
    win_ref,
    half_ref,
    around_ref,
    target_ref,
    cols_ref,
    wide_ref,
):
    features = feat_ref[...]
    nodes = features.shape[1]
    own = (0.5 * nn(win_ref[:, :WIDTH], features)).astype(BF16)
    into = (0.5 * nn(win_ref[:, WIDTH:], features)).astype(BF16)
    from_own = one_hot_rows(src_ref[...], nodes)
    to_target = one_hot_rows(tgt_ref[...], nodes)
    target_ref[...] = to_target
    around_ref[...] = one_hot_rows(src_ref[...] - nodes, around_ref.shape[0])
    half_ref[...] = nn(own, from_own) + nn(into, to_target) + column(0.5 * bias_ref[...], WIDTH)
    wide_ref[0] = wout_ref[...].astype(F32).T.astype(BF16)
    wide_ref[1] = nout_ref[...].astype(F32).T.astype(BF16)
    cols_ref[...] = jnp.broadcast_to(column(0.5 * nbias_ref[...], WIDTH), (WIDTH, nodes))


def level3_kernel(
    feat_ref,
    half_ref,
    around_ref,
    target_ref,
    cols_ref,
    wide_ref,
    h0,
    h1,
    h2,
    h3,
    win_ref,
    nin_ref,
    updated_ref,
):
    features = feat_ref[...]
    nodes = features.shape[1]
    rim = halo_rows((h0, h1, h2, h3))
    near = (0.5 * nt(win_ref[:, :WIDTH], rim)).astype(BF16)
    hidden = half_silu(half_ref[...] + nn(near, around_ref[...])).astype(BF16)
    message = normed(nn(wide_ref[0], hidden), 0).astype(BF16)
    totals = nt(message, target_ref[...])
    joined = jnp.concatenate([features, totals.astype(BF16)], axis=0)
    hidden = half_silu(0.5 * nn(nin_ref[...], joined) + cols_ref[...]).astype(BF16)
    updated = features.astype(F32) + normed(nn(wide_ref[1], hidden), 0)
    wide = jnp.concatenate([updated, jnp.zeros_like(updated)], axis=1)
    updated_ref[...] = wide.T[:nodes].astype(BF16)


def exchange(shared):
    count = lax.axis_size("py")
    ahead = [(k, (k + 1) % count) for k in range(count)]
    along = [lax.ppermute(shared, "py", ahead)]
    along.append(lax.ppermute(shared, "py", [(b, a) for a, b in ahead]))
    across = []
    for first in (0, 1):
        pairs = [(k, k + 1) for k in range(first, lax.axis_size("px") - 1, 2)]
        across.append(lax.ppermute(shared, "px", pairs + [(b, a) for a, b in pairs]))
    return across + along


def fetch(sources, targets, sems):
    copies = [
        pltpu.make_async_copy(source, target, sems.at[k])
        for k, (source, target) in enumerate(zip(sources, targets))
    ]
    for copy in copies:
        copy.start()
    return copies


def call(kernel, outs, scratch, *args, far=(), leave=(), loose=False):
    held, away = pl.BlockSpec(memory_space=pltpu.VMEM), pl.BlockSpec(memory_space=pl.ANY)
    return pl.pallas_call(
        kernel,
        out_shape=[
            (jax.ShapeDtypeStruct if k in leave else pltpu.VMEM)(*out) for k, out in enumerate(outs)
        ],
        in_specs=[away] * len(far) + [held] * len(args),
        out_specs=[away if far and k in leave else held for k in range(len(outs))],
        scratch_shapes=scratch,
        name=kernel.__name__,
    )(*far, *(args if loose else [pltpu.with_memory_space_constraint(arg, pltpu.VMEM) for arg in args]))


def body(
    node_features,
    edge_source,
    edge_target,
    halo_send,
    edge_weight_in,
    edge_bias,
    edge_weight_out,
    node_weight_in,
    node_bias,
    node_weight_out,
    cluster_owner,
    cluster_member,
    coarse_send,
    coarse_source,
    coarse_target,
    coarse_edge_in,
    coarse_edge_bias,
    coarse_edge_out,
    coarse_node_in,
    coarse_node_bias,
    coarse_node_out,
):
    nodes = node_features.shape[0]
    outs = lambda arrays: [(array.shape, array.dtype) for array in arrays]
    dma = pltpu.SemaphoreType.DMA
    features = node_features.T
    (shared,) = call(
        pick_kernel,
        [((halo_send.shape[1], WIDTH), BF16)],
        [],
        halo_send,
        features,
        loose=True,
    )
    rims = exchange(shared)
    held = (
        edge_weight_in.T,
        coarse_send,
        edge_bias[None],
        node_bias[None],
        edge_weight_out,
        node_weight_out,
        node_weight_in.T,
        edge_source,
        edge_target,
        cluster_owner.reshape(1, nodes),
        cluster_member.reshape(1, nodes),
        coarse_source,
        coarse_target,
    )
    own, into, cols, wide, chosen, *held = call(
        prepare_kernel,
        [
            ((WIDTH, nodes), BF16),
            ((WIDTH, nodes), BF16),
            ((2, WIDTH, 128), F32),
            ((2, WIDTH, WIDTH), BF16),
            ((coarse_send.shape[1], CLUST_DEV), BF16),
        ]
        + outs(held),
        [dma((len(held),))],
        features,
        far=held,
    )
    w_in, n_in, source, target, owner, member = held[:1] + held[6:11]
    updated, payload = call(
        fine_kernel,
        [((WIDTH, nodes), BF16), ((OWNERS, WIDTH // 2 + 8, 2 * CLUST_DEV), BF16)],
        [pltpu.VMEM((WIDTH, 1280), BF16), pltpu.VMEM((WIDTH, nodes), F32)],
        features,
        own,
        into,
        cols,
        wide,
        *rims,
        source,
        target,
        w_in,
        n_in,
        owner,
        member,
        leave=(0,),
    )
    parts = lax.all_to_all(payload, "py", 0, 0, tiled=True)
    coarse, coarse_shared = call(
        coarse_kernel,
        [((WIDTH, CLUST_DEV), BF16), ((coarse_send.shape[1], WIDTH), BF16)],
        [],
        parts,
        chosen,
    )
    coarse_rims = exchange(coarse_shared)
    links = coarse_source.shape[1]
    prepared = call(
        prepare3_kernel,
        [
            ((WIDTH, links), F32),
            ((4 * coarse_send.shape[1], links), BF16),
            ((CLUST_DEV, links), BF16),
            ((WIDTH, CLUST_DEV), F32),
            ((2, WIDTH, WIDTH), BF16),
        ],
        [],
        *held[11:],
        coarse_edge_bias[None],
        coarse_node_bias[None],
        coarse_edge_out,
        coarse_node_out,
        coarse,
        coarse_edge_in.T,
    )
    (cluster_updated,) = call(
        level3_kernel,
        [((CLUST_DEV, WIDTH), BF16)],
        [],
        coarse,
        *prepared,
        *coarse_rims,
        coarse_edge_in.T,
        coarse_node_in.T,
        leave=(0,),
    )
    return updated.T, cluster_updated


def solution(mesh):
    split, whole = P(("px", "py"), None), P()
    return jax.shard_map(
        body,
        mesh=mesh,
        in_specs=(split,) * 4
        + (whole,) * 6
        + (split, P(("px", "py")))
        + (split,) * 3
        + (whole,) * 6,
        out_specs=(split, split),
        check_vma=False,
    )
```
